512 devices in a mesh: seq: 128 (over y, z, core), rep: 4 (over x).
Axes of the slice: x: 4, y: 8, z: 8, core: 2. Of those that a mesh axis runs over, the one named last changes fastest.
Arguments:
- points: bfloat16 [65536, 512], P(('rep', 'seq')), parts along dimension 0, may hold values from -6 to 6
- decay_one: float32 [8, 65536], P(None, ('rep', 'seq')), parts along dimension 1, may hold values from -1 to 0
- decay_two: float32 [8, 131072], P(None, ('rep', 'seq')), parts along dimension 1, may hold values from -1 to 0
- block_target: int32 [8192], P('rep'), parts along dimension 0, may hold values from 0 to 4095, as said below
- w_qkv_one: bfloat16 [512, 1536], replicated, may hold values from -0.25 to 0.25
- w_out_one: bfloat16 [512, 512], replicated, may hold values from -0.25 to 0.25
- w_up: bfloat16 [512, 2048], P(None, 'seq'), may hold values from -0.25 to 0.25
- w_down: bfloat16 [2048, 512], P('seq'), may hold values from -0.125 to 0.125
- w_qkv_two: bfloat16 [512, 1536], replicated, may hold values from -0.25 to 0.25
- w_out_two: bfloat16 [512, 512], replicated, may hold values from -0.25 to 0.25
Outputs:
- mixed: bfloat16 [131072, 512], P(('rep', 'seq')), parts along dimension 0
The draws below stay inside these ranges and needn't reach their ends.
There are 4 independent parts, one for each index of `rep`. The reference program is written for one: setup_inputs(seed, part) draws one part's arguments, and reference() takes and returns one part's arrays. A program takes and returns all parts, laid end to end along the dimension named above; an argument that names none is the same for every part. Nothing has to cross between parts.
Inputs may be any that keep to these rules, and one draw needn't show every extreme that they name: `block_target`: entry b is the slot of block b of points; slot g is position g % 32 on device g // 32 of seq, and slots in increasing order give the second sequence. Entries are distinct, every device uses its first slots only, and some device uses all 32. Taken in slot order the blocks go column by column: for one local index j, the j-th block of every device in increasing device order, the columns in some order. At most 1 block of one device go to one device, and some device sends that many to one device.
All inputs are finite; a program needn't handle non-finite values.
Results may differ from the reference program's by a relative error of at most 0.018.
Values may be sent and summed in bfloat16 or wider, within the bound.
No kernel may reach another device: no remote copies, remote signals or barrier semaphores. Data moves between devices by JAX's collectives and lax.ppermute only.
A program may use at most 128 MiB of HBM per device.

```python
import math
import jax
import jax.numpy as jnp
from jax import lax

D = 512
MIXER_STREAMS = 8
HEAD_DIM = 64
FF = 2048
BR = 8
TOK_DEV = 128
BLK_DEV = 16
CAP = 32
TOKENS = 16384
NBLK = 2048
SLOTS = 4096


def decay_law(key, overall_span, group):
    matching_rows = jax.random.split(jax.random.fold_in(key, 7), 8)
    order = jax.random.permutation(matching_rows[0], MIXER_STREAMS)
    slow_count = MIXER_STREAMS // 2
    slow = jnp.zeros((MIXER_STREAMS,), jnp.int32).at[order[:slow_count]].set(1) > 0
    slow_rate = jnp.exp(jax.random.uniform(matching_rows[1], (MIXER_STREAMS,), jnp.float32, math.log(0.08), math.log(0.2))) * math.log(10.0) / TOKENS
    fast_rate = jnp.exp(jax.random.uniform(matching_rows[2], (MIXER_STREAMS,), jnp.float32, math.log(1.0 / 50.0), math.log(1.0 / 30.0)))
    forgetting_rate = jnp.where(slow, slow_rate, fast_rate)
    rough_guess = jax.random.uniform(matching_rows[3], (MIXER_STREAMS, overall_span), jnp.float32, 0.5, 1.5)
    processor_scaling = jnp.exp(jax.random.uniform(matching_rows[4], (overall_span // group,), jnp.float32, math.log(0.6), math.log(1.8)))
    processor_scaling = jnp.repeat(processor_scaling, group)
    initial_bundle = jax.random.randint(matching_rows[5], (MIXER_STREAMS, 1), 0, overall_span)
    subsequent_bundle = (initial_bundle + 1 + jax.random.randint(matching_rows[6], (MIXER_STREAMS, 1), 0, overall_span - 1)) % overall_span
    level_count = jnp.log(jax.random.uniform(matching_rows[7], (MIXER_STREAMS, 2), jnp.float32, 0.5, 0.8))
    position_numbers = lax.broadcasted_iota(jnp.int32, (MIXER_STREAMS, overall_span), 1)
    message_bundles = jnp.where(position_numbers == initial_bundle, level_count[:, :1], 0.0) + jnp.where(position_numbers == subsequent_bundle, level_count[:, 1:], 0.0)
    return -forgetting_rate[:, None] * rough_guess * processor_scaling[None, :] + message_bundles


def draw_decay_one(key, part):
    return decay_law(key, TOKENS, TOK_DEV)


def draw_decay_two(key, part):
    return decay_law(jax.random.fold_in(key, 3), SLOTS * BR, CAP * BR)


def draw_block_target(key, part):
    matching_rows = jax.random.split(jax.random.fold_in(key, 5), 3)
    seq_count = NBLK // BLK_DEV
    column_order = jax.random.permutation(matching_rows[0], BLK_DEV)
    column_rank = jnp.argsort(column_order).astype(jnp.int32)
    pairing = jax.random.permutation(matching_rows[1], seq_count)
    shifts = jax.random.randint(matching_rows[2], (seq_count // 2,), 0, BLK_DEV + 1).at[0].set(BLK_DEV)
    lengths = jnp.zeros((seq_count,), jnp.int32).at[pairing[0::2]].set(BLK_DEV + shifts).at[pairing[1::2]].set(BLK_DEV - shifts)
    ends = jnp.cumsum(lengths)
    starts = ends - lengths
    order_pos = jnp.arange(NBLK, dtype=jnp.int32)
    owner = jnp.sum((ends[None, :] <= order_pos[:, None]).astype(jnp.int32), axis=1)
    slot_of = owner * CAP + order_pos - starts[owner]
    blocks = jnp.arange(NBLK, dtype=jnp.int32)
    where_in = column_rank[blocks % BLK_DEV] * seq_count + blocks // BLK_DEV
    return slot_of[where_in].astype(jnp.int32)


def level_of(key, dims, cuts, least, high):
    def one(position, shards_of):
        draws = jax.random.uniform(jax.random.fold_in(jax.random.fold_in(key, 6), position), (shards_of,), jnp.float32, least / len(cuts), high / len(cuts))
        return jnp.repeat(jnp.exp(draws), dims[position] // shards_of).reshape((-1,) + (1,) * (len(dims) - position - 1))

    loudness = one(*cuts[0])
    for cut in cuts[1:]:
        loudness = loudness * one(*cut)
    return loudness


def centred(own_key, extent, scale, reach, cuts=(), held_as=jnp.bfloat16):
    result = jax.random.normal(own_key, extent, jnp.float32) * scale
    if len(cuts) > 0:
        result = level_of(own_key, extent, cuts, -0.22, 0.18) * result
    return jnp.clip(result, min=-reach, max=reach).astype(held_as)


def setup_inputs(seed: int = 0, part: int = 0) -> dict:
    key_list = jax.random.split(jax.random.key(seed), 11)
    part_splits = jax.random.split(jax.random.fold_in(key_list[10], part), 11)
    return {
        "points": centred(part_splits[0], (TOKENS, D), 1.0, 6.0, ((0, 128),)),
        "decay_one": draw_decay_one(jax.random.fold_in(jax.random.fold_in(key_list[10], part), 71), part),
        "decay_two": draw_decay_two(jax.random.fold_in(jax.random.fold_in(key_list[10], part), 71), part),
        "block_target": draw_block_target(jax.random.fold_in(jax.random.fold_in(key_list[10], part), 71), part),
        "w_qkv_one": centred(key_list[4], (D, 3 * D), D ** -0.5, 0.25),
        "w_out_one": centred(key_list[5], (D, D), D ** -0.5, 0.25),
        "w_up": centred(key_list[6], (D, FF), D ** -0.5, 0.25, ((1, 128),)),
        "w_down": centred(key_list[7], (FF, D), FF ** -0.5, 0.125, ((0, 128),)),
        "w_qkv_two": centred(key_list[8], (D, 3 * D), D ** -0.5, 0.25),
        "w_out_two": centred(key_list[9], (D, D), D ** -0.5, 0.25),
    }


epsilon = 1e-05
highest = lax.Precision.HIGHEST

def rms_rows(inputs):
    wide = inputs.astype(jnp.float32)
    return wide * lax.rsqrt(lax.optimization_barrier(jnp.mean(wide * wide, axis=-1, keepdims=True)) + epsilon)

def project(inputs, weight):
    normed = rms_rows(inputs).astype(jnp.bfloat16)
    joined = jnp.dot(normed, weight, preferred_element_type=jnp.float32)
    column = lax.broadcasted_iota(jnp.int32, (1, 3 * D), 1)
    scaled = jnp.where(column < D, joined * HEAD_DIM ** (-0.5), joined)
    return scaled.astype(jnp.bfloat16)

def block_summary(key_rows, values, decay):
    cumulative = jnp.cumsum(decay, axis=1)
    decay_total = cumulative[:, -1]
    weighted = key_rows.astype(jnp.float32) * jnp.exp(decay_total[:, None] - cumulative)[:, :, None]
    state_sum = jnp.einsum('hsd,hse->hde', weighted, values.astype(jnp.float32), precision=highest)
    return (cumulative, decay_total, state_sum)

def block_output(queries, key_rows, values, cumulative, entering):
    span = queries.shape[1]
    causal = (lax.broadcasted_iota(jnp.int32, (span, span), 0) >= lax.broadcasted_iota(jnp.int32, (span, span), 1))[None]
    gap = cumulative[:, :, None] - cumulative[:, None, :]
    weight = jnp.where(causal, jnp.exp(jnp.where(causal, gap, 0.0)), 0.0)
    scores = jnp.einsum('htd,hsd->hts', queries.astype(jnp.float32), key_rows.astype(jnp.float32))
    weighted = (scores * weight).astype(jnp.bfloat16)
    inner = jnp.einsum('hts,hse->hte', weighted.astype(jnp.float32), values.astype(jnp.float32))
    carried = jnp.einsum('htd,hde->hte', queries.astype(jnp.float32), entering, precision=highest)
    summed = inner + carried * jnp.exp(cumulative)[:, :, None]
    return summed * lax.rsqrt(lax.optimization_barrier(jnp.mean(summed * summed, axis=-1, keepdims=True)) + epsilon)

def attend_all(joined, decay):
    total_rows = joined.shape[0]
    span = math.gcd(total_rows, 512)
    count = total_rows // span

    def heads_blocks(matrix):
        return matrix.reshape(count, span, MIXER_STREAMS, HEAD_DIM).transpose(0, 2, 1, 3)
    queries = heads_blocks(joined[:, :D])
    key_rows = heads_blocks(joined[:, D:2 * D])
    values = heads_blocks(joined[:, 2 * D:])
    decay_blocks = decay.reshape(MIXER_STREAMS, count, span).transpose(1, 0, 2)

    def advance(carry, pieces):
        query_block, key_block, value_block, decay_block = pieces
        cumulative, decay_total, state_sum = block_summary(key_block, value_block, decay_block)
        output = block_output(query_block, key_block, value_block, cumulative, carry)
        carry = carry * jnp.exp(decay_total)[:, None, None] + state_sum
        return (carry, output.astype(jnp.bfloat16))
    start = jnp.zeros((MIXER_STREAMS, HEAD_DIM, HEAD_DIM), jnp.float32)
    _, outputs = lax.scan(advance, start, (queries, key_rows, values, decay_blocks))
    return outputs.transpose(0, 2, 1, 3).reshape(total_rows, D)

def reference(points, decay_one, decay_two, block_target, w_qkv_one, w_out_one, w_up, w_down, w_qkv_two, w_out_two):
    joined = project(points, w_qkv_one)
    attended = attend_all(joined, decay_one)
    first = (points.astype(jnp.float32) + jnp.dot(attended, w_out_one, preferred_element_type=jnp.float32)).astype(jnp.bfloat16)
    normed = rms_rows(first).astype(jnp.bfloat16)
    hidden = jax.nn.gelu(jnp.dot(normed, w_up, preferred_element_type=jnp.float32), approximate=True).astype(jnp.bfloat16)
    layer_out = (first.astype(jnp.float32) + jnp.dot(hidden, w_down, preferred_element_type=jnp.float32)).astype(jnp.bfloat16)
    blocks = layer_out.reshape(NBLK, BR, D)
    placed = jnp.zeros((SLOTS, BR, D), jnp.bfloat16).at[block_target].set(blocks).reshape(SLOTS * BR, D)
    used = jnp.zeros((SLOTS,), jnp.float32).at[block_target].set(1.0)
    decay_mask = jnp.repeat(used, BR)
    joined_two = project(placed, w_qkv_two)
    attended_two = attend_all(joined_two, decay_two * decay_mask[None, :])
    return (placed.astype(jnp.float32) + jnp.dot(attended_two, w_out_two, preferred_element_type=jnp.float32)).astype(jnp.bfloat16)
```

```python
import jax
import jax.numpy as jnp
from jax import lax
from jax.experimental import pallas as pl
from jax.experimental.pallas import tpu as pltpu
from jax.sharding import Mesh
from jax.sharding import PartitionSpec as P

D = 512
HEADS = 8
HEAD_DIM = 64
PAIRS = HEADS // 2
BR = 8
CAP = 32
SEQ = ("seq_0", "seq_1", "seq_2")
ROW = ("seq_1", "seq_2")
REP_SEQ = ("rep", "seq_0", "seq_1", "seq_2")
EPS = 1e-05
F32 = jnp.float32
BF16 = jnp.bfloat16
DIRECT = False

NN = (((1,), (0,)), ((), ()))
NT = (((1,), (1,)), ((), ()))
TN = (((0,), (0,)), ((), ()))


def dot(a, b, dims=NN):
    return lax.dot_general(a, b, dims, preferred_element_type=F32)


def iota(shape, dim):
    return lax.broadcasted_iota(jnp.int32, shape, dim)


def ones_where(cond):
    return jnp.where(cond, 1.0, 0.0).astype(BF16)


def halves(x):
    high = x.astype(BF16)
    return high, (x - high.astype(F32)).astype(BF16)


def thirds(x):
    high, rest = x.astype(BF16), x - x.astype(BF16).astype(F32)
    middle, low = halves(rest)
    return high, middle, low


def rms_rows(wide):
    return wide * lax.rsqrt(jnp.mean(wide * wide, axis=-1, keepdims=True) + EPS)


def project(wide, weight):
    normed = rms_rows(wide).astype(BF16)
    joined = dot(normed, weight)
    return jnp.concatenate(
        [(joined[:, :D] * HEAD_DIM ** (-0.5)).astype(BF16), joined[:, D:].astype(BF16)], axis=1
    )


def running_sums(decay):
    rows = decay.shape[1]
    parts = thirds(decay)
    upto = ones_where(iota((rows, rows), 0) >= iota((rows, rows), 1))
    by_head = sum(dot(part, upto, NT) for part in parts)
    by_row = sum(dot(upto, part, NT) for part in parts)
    return by_head, by_row


def pair_lanes(columns, pair):
    rows = columns.shape[0]
    first = iota((rows, 2 * HEAD_DIM), 1) < HEAD_DIM
    return jnp.where(
        first, columns[:, 2 * pair : 2 * pair + 1], columns[:, 2 * pair + 1 : 2 * pair + 2]
    )


def pack_state(qkv, by_row):
    rows = qkv.shape[0]
    total = by_row[rows - 1 : rows]
    weight = jnp.exp(total - by_row)
    lane = iota((HEAD_DIM, 128), 1)
    place = iota((128, HEAD_DIM), 0)
    spread = ones_where((place % 4 < 2) & (iota((128, HEAD_DIM), 1) == (place // 4) * 2 + place % 4))
    kind = iota((128, 128), 0) % 4
    packed = []
    for p in range(PAIRS):
        keys = qkv[:, D + 128 * p : D + 128 * (p + 1)].astype(F32) * pair_lanes(weight, p)
        values = qkv[:, 2 * D + 128 * p : 2 * D + 128 * (p + 1)]
        high, low = halves(keys)
        both = dot(high, values, TN) + dot(low, values, TN)
        state = jnp.where(lane < HEAD_DIM, both[:HEAD_DIM], both[HEAD_DIM:]).astype(BF16)
        high, low = halves(pair_lanes(total, p))
        piece = dot(spread, state)
        piece = jnp.where(kind == 2, high.astype(F32), piece)
        piece = jnp.where(kind == 3, low.astype(F32), piece)
        packed.append(piece.astype(BF16))
    return jnp.concatenate(packed, axis=0)


def front(points, weight, decay):
    qkv = project(points[...].astype(F32), weight[...])
    by_head, by_row = running_sums(decay[...])
    return qkv, pack_state(qkv, by_row)


def prefix(received):
    rows = received[...]
    total = rows.shape[0]
    devices = total // 4
    shape = (2 * devices, total)
    target, source = iota(shape, 0) // 2, iota(shape, 1) // 4
    part = iota(shape, 1) % 4
    earlier = source < target
    between = ones_where((part >= 2) & earlier)
    mask = earlier & (part == iota(shape, 0) % 2)
    later = iota((total, total), 0) // 4 > iota((total, total), 1) // 4
    outs = []
    for half in range(2):
        decay = rows[:, half * HEAD_DIM : half * HEAD_DIM + 1].astype(F32)
        gap = dot(between, jnp.where(later, decay, 0.0).astype(BF16))
        weight = jnp.where(mask, jnp.exp(gap), 0.0)
        high, low = halves(weight)
        outs.append(dot(high, rows) + dot(low, rows))
    lane = iota(outs[0].shape, 1)
    return jnp.where(lane < HEAD_DIM, outs[0], outs[1]).astype(BF16)


def attend(qkv, by_head, by_row, entering):
    rows = qkv.shape[0]
    causal = iota((rows, rows), 0) >= iota((rows, rows), 1)
    lanes = iota((1, 128), 1)
    sides = (ones_where(lanes < HEAD_DIM), ones_where(lanes >= HEAD_DIM))
    same = ones_where(iota((128, 128), 0) // HEAD_DIM == iota((128, 128), 1) // HEAD_DIM)
    first = iota((rows, 128), 1) < HEAD_DIM
    grown = jnp.exp(by_row)
    attended = []
    for p in range(PAIRS):
        queries = qkv[:, 128 * p : 128 * (p + 1)]
        keys = qkv[:, D + 128 * p : D + 128 * (p + 1)]
        values = qkv[:, 2 * D + 128 * p : 2 * D + 128 * (p + 1)]
        state = entering[HEAD_DIM * p : HEAD_DIM * (p + 1)]
        state = jnp.concatenate([state * sides[0], state * sides[1]], axis=0)
        carried = dot(queries, state) * pair_lanes(grown, p)
        inner = []
        for side in range(2):
            h = 2 * p + side
            scores = dot(queries * sides[side], keys, NT)
            gap = by_row[:, h : h + 1] - by_head[h : h + 1, :]
            weighted = scores * jnp.exp(jnp.where(causal, gap, -1e30))
            inner.append(dot(weighted.astype(BF16), values))
        summed = jnp.where(first, inner[0], inner[1]) + carried
        high, low = halves(summed * summed)
        mean = (dot(high, same) + dot(low, same)) * (1.0 / HEAD_DIM)
        attended.append((summed * lax.rsqrt(mean + EPS)).astype(BF16))
    return jnp.concatenate(attended, axis=1)


def picked(meta, base, count, group):
    return sum(jnp.where(group == k, meta[base + k], 0) for k in range(count))


def middle(meta, points, qkv, decay, entering, w_out):
    by_head, by_row = running_sums(decay[...])
    attended = attend(qkv[...], by_head, by_row, entering[...])
    first = (points[...].astype(F32) + dot(attended, w_out[...])).astype(BF16)
    shape = (256, 128)
    place, column = iota(shape, 0), iota(shape, 1)
    begin = picked_strided(meta, 0, place // 32)
    end = picked_strided(meta, 16, place // 32)
    where = begin + ((meta[160] - begin) & 127) + 128 * ((place // BR) & 3)
    block = picked(meta, 144, 16, where >> 7)
    chosen = (where < end) & (column == block * BR + (place & 7))
    return dot(ones_where(chosen), first).astype(BF16)


def picked_strided(meta, shift, group):
    return sum(jnp.where(group == k, meta[shift + 16 * k], 0) for k in range(8))


def across(meta, arrived):
    shape = (256, 256)
    place, column = iota(shape, 0), iota(shape, 1)
    base = meta[161]
    begin = sum(jnp.where(place // 16 == k, meta[base + k], 0) for k in range(16))
    end = sum(jnp.where(place // 16 == k, meta[base + k + 1], 0) for k in range(16))
    where = begin + ((meta[162] - begin) & 15) + 16 * ((place // BR) & 1)
    held = ((where & 127) >> 4) * 4 + ((where - meta[base]) >> 7)
    chosen = (where < end) & (column == held * BR + (place & 7))
    return dot(ones_where(chosen), arrived[...]).astype(BF16)


def second(meta, arrived, weights, w_qkv, decay):
    shape = (256, 256)
    place, column = iota(shape, 0), iota(shape, 1)
    begin = meta[meta[160]]
    used = meta[meta[160] + 1] - begin
    slot = place // BR
    held = ((begin + slot) & 15) * 2 + slot // 16
    chosen = (slot < used) & (column == held * BR + (place & 7))
    first = dot(ones_where(chosen), arrived[...])
    normed = rms_rows(first).astype(BF16)
    hidden = jax.nn.gelu(dot(normed, weights[:, :D], NT), approximate=True).astype(BF16)
    placed = (first + dot(hidden, weights[:, D:])).astype(BF16)
    qkv = project(placed.astype(F32), w_qkv[...])
    kept = jnp.where(iota(decay.shape, 1) < BR * used, decay[...], 0.0)
    by_head, by_row = running_sums(kept)
    return placed, qkv, kept, pack_state(qkv, by_row)


def last(placed, qkv, decay, entering, w_out):
    by_head, by_row = running_sums(decay[...])
    attended = attend(qkv[...], by_head, by_row, entering[...])
    return (placed[...].astype(F32) + dot(attended, w_out[...])).astype(BF16)


def kernel_call(function, outs, *args, scalars=0):
    if DIRECT:
        return function(*args)
    count = len(args)

    def body(*refs):
        results = function(*refs[:count])
        if len(outs) == 1:
            results = (results,)
        for ref, value in zip(refs[count:], results):
            ref[...] = value

    smem = pl.BlockSpec(memory_space=pltpu.SMEM)
    vmem = pl.BlockSpec(memory_space=pltpu.VMEM)
    result = pl.pallas_call(
        body,
        out_shape=[jax.ShapeDtypeStruct(shape, kind) for shape, kind in outs],
        in_specs=[smem] * scalars + [vmem] * (count - scalars),
        out_specs=[vmem] * len(outs),
        name=function.__name__,
    )(*args)
    return result[0] if len(outs) == 1 else result


def whole(x, axes, pieces):
    split = x.reshape(pieces, x.shape[0] // pieces, x.shape[1])
    return lax.all_to_all(split, axes, split_axis=0, concat_axis=0, tiled=True).reshape(x.shape)


def shards(
    points,
    decay_one,
    decay_two,
    block_target,
    w_qkv_one,
    w_out_one,
    w_up,
    w_down,
    w_qkv_two,
    w_out_two,
):
    position = lax.axis_index(SEQ)
    joined = jnp.concatenate([w_up.T, w_down], axis=1)
    weights = lax.all_gather(joined, SEQ, axis=0, tiled=True)

    limits = CAP * iota((144, 1), 0)
    starts = jnp.sum((block_target[None, :] < limits).astype(jnp.int32), axis=1)
    own = block_target[:16]
    rank = jnp.sum((own[None, :] < own[:, None]).astype(jnp.int32), axis=1)
    order = jnp.sum(jnp.where(rank[None, :] == iota((16, 16), 0), iota((16, 16), 1), 0), axis=1)
    here = jnp.stack([position, position // 16 * 16, position % 16]).astype(jnp.int32)
    meta = jnp.concatenate([starts, order, here])

    qkv, sent = kernel_call(
        front, [((128, 3 * D), BF16), ((512, 128), BF16)], points, w_qkv_one, decay_one
    )
    received = whole(sent, SEQ, 128)
    summed = kernel_call(prefix, [((256, 128), BF16)], received)
    entering = whole(summed, SEQ, 128)
    outgoing = kernel_call(
        middle,
        [((256, D), BF16)],
        meta,
        points,
        qkv,
        decay_one,
        entering,
        w_out_one,
        scalars=1,
    )
    arrived = whole(outgoing, "seq_0", 8)
    outgoing = kernel_call(across, [((256, D), BF16)], meta, arrived, scalars=1)
    arrived = whole(outgoing, ROW, 16)
    placed, qkv, decay, sent = kernel_call(
        second,
        [((256, D), BF16), ((256, 3 * D), BF16), ((HEADS, 256), F32), ((512, 128), BF16)],
        meta,
        arrived,
        weights,
        w_qkv_two,
        decay_two,
        scalars=1,
    )
    received = whole(sent, SEQ, 128)
    summed = kernel_call(prefix, [((256, 128), BF16)], received)
    entering = whole(summed, SEQ, 128)
    return kernel_call(last, [((256, D), BF16)], placed, qkv, decay, entering, w_out_two)


def solution(mesh):
    split = Mesh(
        mesh.devices.reshape(8, 8, 2, mesh.shape["rep"]), ("seq_0", "seq_1", "seq_2", "rep")
    )
    placed = (
        P(REP_SEQ, None),
        P(None, REP_SEQ),
        P(None, REP_SEQ),
        P("rep"),
        P(),
        P(),
        P(None, SEQ),
        P(SEQ, None),
        P(),
        P(),
    )
    return jax.shard_map(
        shards, mesh=split, in_specs=placed, out_specs=P(REP_SEQ, None), check_vma=False
    )
```

```python
import jax
import jax.numpy as jnp
from jax import lax
from jax.experimental import pallas as pl
from jax.experimental.pallas import tpu as pltpu
from jax.sharding import Mesh
from jax.sharding import PartitionSpec as P

D = 512
HEADS = 8
HEAD_DIM = 64
PAIRS = HEADS // 2
BR = 8
CAP = 32
SEQ = ("seq_0", "seq_1", "seq_2")
CHIPS = ("seq_0", "seq_1")
REP_SEQ = ("rep", "seq_0", "seq_1", "seq_2")
EPS = 1e-05
F32 = jnp.float32
BF16 = jnp.bfloat16
DIRECT = False

NN = (((1,), (0,)), ((), ()))
NT = (((1,), (1,)), ((), ()))
TN = (((0,), (0,)), ((), ()))


def dot(a, b, dims=NN):
    return lax.dot_general(a, b, dims, preferred_element_type=F32)


def iota(shape, dim):
    return lax.broadcasted_iota(jnp.int32, shape, dim)


def ones_where(cond):
    return jnp.where(cond, 1.0, 0.0).astype(BF16)


def halves(x):
    high = x.astype(BF16)
    return high, (x - high.astype(F32)).astype(BF16)


def thirds(x):
    high, rest = x.astype(BF16), x - x.astype(BF16).astype(F32)
    middle, low = halves(rest)
    return high, middle, low


def rms_rows(wide):
    return wide * lax.rsqrt(jnp.mean(wide * wide, axis=-1, keepdims=True) + EPS)


def project(wide, weight):
    normed = rms_rows(wide).astype(BF16)
    joined = dot(normed, weight)
    return jnp.concatenate(
        [(joined[:, :D] * HEAD_DIM ** (-0.5)).astype(BF16), joined[:, D:].astype(BF16)], axis=1
    )


def running_sums(decay):
    rows = decay.shape[1]
    parts = thirds(decay)
    upto = ones_where(iota((rows, rows), 0) >= iota((rows, rows), 1))
    by_head = sum(dot(part, upto, NT) for part in parts)
    by_row = sum(dot(upto, part, NT) for part in parts)
    return by_head, by_row


def pair_lanes(columns, pair):
    rows = columns.shape[0]
    first = iota((rows, 2 * HEAD_DIM), 1) < HEAD_DIM
    return jnp.where(
        first, columns[:, 2 * pair : 2 * pair + 1], columns[:, 2 * pair + 1 : 2 * pair + 2]
    )


def pack_state(qkv, by_row):
    rows = qkv.shape[0]
    total = by_row[rows - 1 : rows]
    weight = jnp.exp(total - by_row)
    lane = iota((HEAD_DIM, 128), 1)
    place = iota((128, HEAD_DIM), 0)
    spread = ones_where((place % 4 < 2) & (iota((128, HEAD_DIM), 1) == (place // 4) * 2 + place % 4))
    kind = iota((128, 128), 0) % 4
    packed = []
    for p in range(PAIRS):
        keys = qkv[:, D + 128 * p : D + 128 * (p + 1)].astype(F32) * pair_lanes(weight, p)
        values = qkv[:, 2 * D + 128 * p : 2 * D + 128 * (p + 1)]
        high, low = halves(keys)
        both = dot(high, values, TN) + dot(low, values, TN)
        state = jnp.where(lane < HEAD_DIM, both[:HEAD_DIM], both[HEAD_DIM:]).astype(BF16)
        high, low = halves(pair_lanes(total, p))
        piece = dot(spread, state)
        piece = jnp.where(kind == 2, high.astype(F32), piece)
        piece = jnp.where(kind == 3, low.astype(F32), piece)
        packed.append(piece.astype(BF16))
    return jnp.concatenate(packed, axis=0)


def front(points, weight, decay):
    qkv = project(points[...].astype(F32), weight[...])
    by_head, by_row = running_sums(decay[...])
    return qkv, pack_state(qkv, by_row)


def prefix(received):
    rows = received[...]
    total = rows.shape[0]
    devices = total // 4
    shape = (2 * devices, total)
    target, source = iota(shape, 0) // 2, iota(shape, 1) // 4
    part = iota(shape, 1) % 4
    earlier = source < target
    between = ones_where((part >= 2) & earlier)
    mask = earlier & (part == iota(shape, 0) % 2)
    later = iota((total, total), 0) // 4 > iota((total, total), 1) // 4
    outs = []
    for half in range(2):
        decay = rows[:, half * HEAD_DIM : half * HEAD_DIM + 1].astype(F32)
        gap = dot(between, jnp.where(later, decay, 0.0).astype(BF16))
        weight = jnp.where(mask, jnp.exp(gap), 0.0)
        high, low = halves(weight)
        outs.append(dot(high, rows) + dot(low, rows))
    lane = iota(outs[0].shape, 1)
    return jnp.where(lane < HEAD_DIM, outs[0], outs[1]).astype(BF16)


def attend(qkv, by_head, by_row, entering):
    rows = qkv.shape[0]
    causal = iota((rows, rows), 0) >= iota((rows, rows), 1)
    lanes = iota((1, 128), 1)
    sides = (ones_where(lanes < HEAD_DIM), ones_where(lanes >= HEAD_DIM))
    same = ones_where(iota((128, 128), 0) // HEAD_DIM == iota((128, 128), 1) // HEAD_DIM)
    first = iota((rows, 128), 1) < HEAD_DIM
    grown = jnp.exp(by_row)
    attended = []
    for p in range(PAIRS):
        queries = qkv[:, 128 * p : 128 * (p + 1)]
        keys = qkv[:, D + 128 * p : D + 128 * (p + 1)]
        values = qkv[:, 2 * D + 128 * p : 2 * D + 128 * (p + 1)]
        state = entering[HEAD_DIM * p : HEAD_DIM * (p + 1)]
        state = jnp.concatenate([state * sides[0], state * sides[1]], axis=0)
        carried = dot(queries, state) * pair_lanes(grown, p)
        inner = []
        for side in range(2):
            h = 2 * p + side
            scores = dot(queries * sides[side], keys, NT)
            gap = by_row[:, h : h + 1] - by_head[h : h + 1, :]
            weighted = scores * jnp.exp(jnp.where(causal, gap, -1e30))
            inner.append(dot(weighted.astype(BF16), values))
        summed = jnp.where(first, inner[0], inner[1]) + carried
        high, low = halves(summed * summed)
        mean = (dot(high, same) + dot(low, same)) * (1.0 / HEAD_DIM)
        attended.append((summed * lax.rsqrt(mean + EPS)).astype(BF16))
    return jnp.concatenate(attended, axis=1)


def middle(chips, points, qkv, decay, entering, w_out):
    by_head, by_row = running_sums(decay[...])
    attended = attend(qkv[...], by_head, by_row, entering[...])
    first = (points[...].astype(F32) + dot(attended, w_out[...])).astype(BF16)
    shape = (512, 128)
    place, column = iota(shape, 0), iota(shape, 1)
    chosen = (place // BR == chips[...]) & ((place & 7) == (column & 7))
    return dot(ones_where(chosen), first).astype(BF16)


def across(meta, arrived):
    shape = (256, 512)
    place, column = iota(shape, 0), iota(shape, 1)
    begin = jnp.where(place < 128, meta[0], meta[1])
    end = jnp.where(place < 128, meta[1], meta[2])
    where = begin + ((meta[3] - begin) & 1) + 2 * ((place // BR) & 15)
    held = (where & 127) >> 1
    chosen = (where < end) & (column == held * BR + (place & 7))
    return dot(ones_where(chosen), arrived[...]).astype(BF16)


def second(meta, arrived, weights, others, w_qkv, decay):
    shape = (256, 256)
    place, column = iota(shape, 0), iota(shape, 1)
    begin = jnp.where(meta[3] == 0, meta[0], meta[1])
    used = jnp.where(meta[3] == 0, meta[1], meta[2]) - begin
    slot = place // BR
    held = ((begin + slot) & 1) * 16 + slot // 2
    chosen = (slot < used) & (column == held * BR + (place & 7))
    first = dot(ones_where(chosen), arrived[...])
    normed = rms_rows(first).astype(BF16)
    rows = weights.shape[0] // 2
    down_sum = first
    for part in (weights, others):
        up = part[pl.ds(pl.multiple_of(meta[4], rows), rows), :]
        down = part[pl.ds(pl.multiple_of(rows - meta[4], rows), rows), :]
        hidden = jax.nn.gelu(dot(normed, up, NT), approximate=True).astype(BF16)
        down_sum = down_sum + dot(hidden, down)
    placed = down_sum.astype(BF16)
    qkv = project(placed.astype(F32), w_qkv[...])
    kept = jnp.where(iota(decay.shape, 1) < BR * used, decay[...], 0.0)
    by_head, by_row = running_sums(kept)
    return placed, qkv, kept, pack_state(qkv, by_row)


def last(placed, qkv, decay, entering, w_out):
    by_head, by_row = running_sums(decay[...])
    attended = attend(qkv[...], by_head, by_row, entering[...])
    return (placed[...].astype(F32) + dot(attended, w_out[...])).astype(BF16)


def kernel_call(function, outs, *args, scalars=0):
    if DIRECT:
        return function(*args)
    count = len(args)

    def body(*refs):
        results = function(*refs[:count])
        if len(outs) == 1:
            results = (results,)
        for ref, value in zip(refs[count:], results):
            ref[...] = value

    smem = pl.BlockSpec(memory_space=pltpu.SMEM)
    vmem = pl.BlockSpec(memory_space=pltpu.VMEM)
    result = pl.pallas_call(
        body,
        out_shape=[jax.ShapeDtypeStruct(shape, kind) for shape, kind in outs],
        in_specs=[smem] * scalars + [vmem] * (count - scalars),
        out_specs=[vmem] * len(outs),
        name=function.__name__,
    )(*args)
    return result[0] if len(outs) == 1 else result


def whole(x, axes, pieces):
    split = x.reshape(pieces, x.shape[0] // pieces, x.shape[1])
    return lax.all_to_all(split, axes, split_axis=0, concat_axis=0, tiled=True).reshape(x.shape)


def shards(
    points,
    decay_one,
    decay_two,
    block_target,
    w_qkv_one,
    w_out_one,
    w_up,
    w_down,
    w_qkv_two,
    w_out_two,
):
    plane = lax.axis_index("rep")
    half = plane // 2 * BR
    mine = jnp.where(
        plane % 2 == 0,
        lax.dynamic_slice_in_dim(w_up, half, BR, 1).T,
        lax.dynamic_slice_in_dim(w_down, half, BR, 0),
    )
    quarter = lax.all_to_all(
        jnp.broadcast_to(mine[None], (64, BR, D)), CHIPS, split_axis=0, concat_axis=0, tiled=True
    ).reshape(64 * BR, D)
    position = lax.axis_index(SEQ)
    core = lax.axis_index("seq_2")
    limits = CAP * (position - core + iota((3, 1), 0))
    starts = jnp.sum((block_target[None, :] < limits).astype(jnp.int32), axis=1)
    meta = jnp.concatenate([starts, jnp.stack([core, plane % 2 * 1024]).astype(jnp.int32)])
    own = lax.dynamic_slice_in_dim(block_target, position * 16, 16)
    chips = jnp.repeat(own // (2 * CAP), BR)[None, :]

    qkv, sent = kernel_call(
        front, [((128, 3 * D), BF16), ((512, 128), BF16)], points, w_qkv_one, decay_one
    )
    quarter, sent = lax.optimization_barrier((quarter, sent))
    planes = [
        lax.ppermute(quarter, "rep", [(i, i ^ step) for i in range(4)]) for step in (2, 1, 3)
    ]
    received = whole(sent, SEQ, 128)
    planes, received = lax.optimization_barrier((planes, received))
    summed = kernel_call(prefix, [((256, 128), BF16)], received)
    weights = jnp.concatenate([quarter] + planes, axis=0)
    entering = whole(summed, SEQ, 128)
    weights, entering = lax.optimization_barrier((weights, entering))
    others = lax.ppermute(weights, "seq_2", [(0, 1), (1, 0)])
    outgoing = kernel_call(
        middle, [((512, D), BF16)], chips, points, qkv, decay_one, entering, w_out_one
    )
    arrived = whole(outgoing, CHIPS, 64)
    outgoing = kernel_call(across, [((256, D), BF16)], meta, arrived, scalars=1)
    arrived = whole(outgoing, "seq_2", 2)
    others, arrived = lax.optimization_barrier((others, arrived))
    placed, qkv, decay, sent = kernel_call(
        second,
        [((256, D), BF16), ((256, 3 * D), BF16), ((HEADS, 256), F32), ((512, 128), BF16)],
        meta,
        arrived,
        weights,
        others,
        w_qkv_two,
        decay_two,
        scalars=1,
    )
    received = whole(sent, SEQ, 128)
    summed = kernel_call(prefix, [((256, 128), BF16)], received)
    entering = whole(summed, SEQ, 128)
    return kernel_call(last, [((256, D), BF16)], placed, qkv, decay, entering, w_out_two)


def solution(mesh):
    split = Mesh(
        mesh.devices.reshape(8, 8, 2, mesh.shape["rep"]), ("seq_0", "seq_1", "seq_2", "rep")
    )
    placed = (
        P(REP_SEQ, None),
        P(None, REP_SEQ),
        P(None, REP_SEQ),
        P("rep"),
        P(),
        P(),
        P(None, SEQ),
        P(SEQ, None),
        P(),
        P(),
    )
    return jax.shard_map(
        shards, mesh=split, in_specs=placed, out_specs=P(REP_SEQ, None), check_vma=False
    )
```

```python
import jax
import jax.numpy as jnp
from jax import lax
from jax.experimental import pallas as pl
from jax.experimental.pallas import tpu as pltpu
from jax.sharding import Mesh
from jax.sharding import PartitionSpec as P

D = 512
HEADS = 8
HEAD_DIM = 64
PAIRS = HEADS // 2
BR = 8
CAP = 32
SEQ = ("seq_0", "seq_1", "seq_2")
CHIPS = ("seq_0", "seq_1")
ROW = ("seq_1", "seq_2")
REP_SEQ = ("rep", "seq_0", "seq_1", "seq_2")
EPS = 1e-05
F32 = jnp.float32
BF16 = jnp.bfloat16
DIRECT = False

NN = (((1,), (0,)), ((), ()))
NT = (((1,), (1,)), ((), ()))
TN = (((0,), (0,)), ((), ()))


def dot(a, b, dims=NN):
    return lax.dot_general(a, b, dims, preferred_element_type=F32)


def iota(shape, dim):
    return lax.broadcasted_iota(jnp.int32, shape, dim)


def ones_where(cond):
    return jnp.where(cond, 1.0, 0.0).astype(BF16)


def halves(x):
    high = x.astype(BF16)
    return high, (x - high.astype(F32)).astype(BF16)


def thirds(x):
    high, rest = x.astype(BF16), x - x.astype(BF16).astype(F32)
    middle, low = halves(rest)
    return high, middle, low


def rms_rows(wide):
    return wide * lax.rsqrt(jnp.mean(wide * wide, axis=-1, keepdims=True) + EPS)


def running_sums(decay):
    rows = decay.shape[1]
    parts = thirds(decay)
    upto = ones_where(iota((rows, rows), 0) >= iota((rows, rows), 1))
    by_head = sum(dot(part, upto, NT) for part in parts)
    by_row = sum(dot(upto, part, NT) for part in parts)
    return by_head, by_row


def pair_lanes(columns, pair):
    rows = columns.shape[0]
    first = iota((rows, 2 * HEAD_DIM), 1) < HEAD_DIM
    return jnp.where(
        first, columns[:, 2 * pair : 2 * pair + 1], columns[:, 2 * pair + 1 : 2 * pair + 2]
    )


def pack_state(keys_values, by_row):
    rows = keys_values.shape[0]
    total = by_row[rows - 1 : rows]
    weight = jnp.exp(total - by_row)
    lane = iota((HEAD_DIM, 128), 1)
    place = iota((128, HEAD_DIM), 0)
    spread = ones_where((place % 4 < 2) & (iota((128, HEAD_DIM), 1) == (place // 4) * 2 + place % 4))
    kind = iota((128, 128), 0) % 4
    packed = []
    for p in range(PAIRS):
        keys = keys_values[:, 128 * p : 128 * (p + 1)].astype(F32) * pair_lanes(weight, p)
        values = keys_values[:, D + 128 * p : D + 128 * (p + 1)]
        high, low = halves(keys)
        both = dot(high, values, TN) + dot(low, values, TN)
        state = jnp.where(lane < HEAD_DIM, both[:HEAD_DIM], both[HEAD_DIM:]).astype(BF16)
        high, low = halves(pair_lanes(total, p))
        piece = dot(spread, state)
        piece = jnp.where(kind == 2, high.astype(F32), piece)
        piece = jnp.where(kind == 3, low.astype(F32), piece)
        packed.append(piece.astype(BF16))
    return jnp.concatenate(packed, axis=0)


def front(points, weight, decay):
    normed = rms_rows(points[...].astype(F32)).astype(BF16)
    keys_values = dot(normed, weight[:, D:]).astype(BF16)
    by_row = running_sums(decay[...])[1]
    return normed, keys_values, pack_state(keys_values, by_row)


def prefix(received):
    rows = received[...]
    devices = rows.shape[0] // 4
    square = (devices, devices)
    pick = iota((devices, 4 * devices), 1) - 4 * iota((devices, 4 * devices), 0)
    states = [dot(ones_where(pick == j), rows).astype(BF16) for j in range(2)]
    totals = [dot(ones_where(pick == 2 + j), rows) for j in range(2)]
    earlier = iota(square, 1) < iota(square, 0)
    before = ones_where(earlier)
    later = iota(square, 0) > iota(square, 1)
    outs = []
    for half in range(2):
        gap = sum(
            dot(
                before,
                jnp.where(later, part[:, half * HEAD_DIM : half * HEAD_DIM + 1], 0.0).astype(BF16),
            )
            for part in totals
        )
        high, low = halves(jnp.where(earlier, jnp.exp(gap), 0.0))
        outs.append([dot(high, state) + dot(low, state) for state in states])
    lane = iota(square, 1) < HEAD_DIM
    back = iota((2 * devices, devices), 0) - 2 * iota((2 * devices, devices), 1)
    return sum(
        dot(ones_where(back == j), jnp.where(lane, outs[0][j], outs[1][j]).astype(BF16))
        for j in range(2)
    ).astype(BF16)


def inner(normed, weight, keys_values, decay):
    by_head, by_row = running_sums(decay[...])
    queries = (dot(normed[...], weight[:, :D]) * HEAD_DIM ** (-0.5)).astype(BF16)
    rows = queries.shape[0]
    causal = iota((rows, rows), 0) >= iota((rows, rows), 1)
    lanes = iota((1, 128), 1)
    sides = (ones_where(lanes < HEAD_DIM), ones_where(lanes >= HEAD_DIM))
    first = iota((rows, 128), 1) < HEAD_DIM
    summed = []
    for p in range(PAIRS):
        query = queries[:, 128 * p : 128 * (p + 1)]
        keys = keys_values[:, 128 * p : 128 * (p + 1)]
        values = keys_values[:, D + 128 * p : D + 128 * (p + 1)]
        both = []
        for side in range(2):
            h = 2 * p + side
            scores = dot(query * sides[side], keys, NT)
            gap = by_row[:, h : h + 1] - by_head[h : h + 1, :]
            weighted = scores * jnp.exp(jnp.where(causal, gap, -1e30))
            both.append(dot(weighted.astype(BF16), values))
        summed.append(jnp.where(first, both[0], both[1]))
    return queries, jnp.concatenate(summed, axis=1), jnp.exp(by_row)


def attended(queries, summed, grown, entering):
    lanes = iota((1, 128), 1)
    sides = (ones_where(lanes < HEAD_DIM), ones_where(lanes >= HEAD_DIM))
    same = ones_where(iota((128, 128), 0) // HEAD_DIM == iota((128, 128), 1) // HEAD_DIM)
    outs = []
    for p in range(PAIRS):
        state = entering[HEAD_DIM * p : HEAD_DIM * (p + 1), :]
        state = jnp.concatenate([state * sides[0], state * sides[1]], axis=0)
        carried = dot(queries[:, 128 * p : 128 * (p + 1)], state) * pair_lanes(grown[...], p)
        number = summed[:, 128 * p : 128 * (p + 1)] + carried
        high, low = halves(number * number)
        mean = (dot(high, same) + dot(low, same)) * (1.0 / HEAD_DIM)
        outs.append((number * lax.rsqrt(mean + EPS)).astype(BF16))
    return jnp.concatenate(outs, axis=1)


def middle(chips, points, queries, summed, grown, entering, w_out):
    mixed = dot(attended(queries, summed, grown, entering), w_out[...])
    first = (points[...].astype(F32) + mixed).astype(BF16)
    shape = (512, 128)
    place, column = iota(shape, 0), iota(shape, 1)
    chosen = (place // BR == chips[...]) & ((place & 7) == (column & 7))
    return dot(ones_where(chosen), first).astype(BF16)


def across(meta, arrived):
    shape = (256, 512)
    place, column = iota(shape, 0), iota(shape, 1)
    begin = jnp.where(place < 128, meta[0], meta[1])
    end = jnp.where(place < 128, meta[1], meta[2])
    where = begin + ((meta[3] - begin) & 1) + 2 * ((place // BR) & 15)
    held = (where & 127) >> 1
    chosen = (where < end) & (column == held * BR + (place & 7))
    return dot(ones_where(chosen), arrived[...]).astype(BF16)


def second(meta, arrived, w_qkv, decay, weights, up=None, down=None, copies=None):
    pieces = []
    if up is None:
        up, down = weights[:, :D], weights[:, D:]
    else:
        for k, buffer in enumerate((up, down)):
            pieces.append(
                pltpu.make_async_copy(weights.at[:, pl.ds(k * D, D)], buffer, copies.at[k])
            )
            pieces[k].start()
    shape = (256, 256)
    place, column = iota(shape, 0), iota(shape, 1)
    begin = jnp.where(meta[3] == 0, meta[0], meta[1])
    used = jnp.where(meta[3] == 0, meta[1], meta[2]) - begin
    slot = place // BR
    held = ((begin + slot) & 1) * 16 + slot // 2
    chosen = (slot < used) & (column == held * BR + (place & 7))
    kept = jnp.where(iota(decay.shape, 1) < BR * used, decay[...], 0.0)
    by_row = running_sums(kept)[1]
    first = dot(ones_where(chosen), arrived[...])
    normed = rms_rows(first).astype(BF16)
    if pieces:
        pieces[0].wait()
    hidden = jax.nn.gelu(dot(normed, up[...], NT), approximate=True).astype(BF16)
    if pieces:
        pieces[1].wait()
    placed = (first + dot(hidden, down[...])).astype(BF16)
    normed = rms_rows(placed.astype(F32)).astype(BF16)
    keys_values = dot(normed, w_qkv[:, D:]).astype(BF16)
    return placed, normed, keys_values, kept, pack_state(keys_values, by_row)


def last(placed, queries, summed, grown, entering, w_out):
    mixed = dot(attended(queries, summed, grown, entering), w_out[...])
    return (placed[...].astype(F32) + mixed).astype(BF16)


def kernel_call(function, outs, *args, scalars=0, loose=(), outside=(), streamed=(), scratch=()):
    if DIRECT:
        return function(*args)
    count = len(args)

    def body(*refs):
        results = function(*refs[:count], *refs[count + len(outs) :])
        if len(outs) == 1:
            results = (results,)
        for ref, value in zip(refs[count:], results):
            ref[...] = value

    def spec(k):
        if k < scalars:
            return pl.BlockSpec(memory_space=pltpu.SMEM)
        return pl.BlockSpec(memory_space=pltpu.HBM if k in streamed else pltpu.VMEM)

    args = [
        arg
        if k < scalars or k in loose
        else pltpu.with_memory_space_constraint(
            arg, pltpu.HBM if k in streamed + outside else pltpu.VMEM
        )
        for k, arg in enumerate(args)
    ]
    result = pl.pallas_call(
        body,
        compiler_params=pltpu.CompilerParams(vmem_limit_bytes=32 << 20),
        out_shape=[jax.ShapeDtypeStruct(shape, kind) for shape, kind in outs],
        in_specs=[spec(k) for k in range(count)],
        out_specs=[pl.BlockSpec(memory_space=pltpu.VMEM)] * len(outs),
        scratch_shapes=list(scratch),
        name=function.__name__,
    )(*args)
    return result[0] if len(outs) == 1 else result


def whole(x, axes, pieces):
    split = x.reshape(pieces, x.shape[0] // pieces, x.shape[1])
    return lax.all_to_all(split, axes, split_axis=0, concat_axis=0, tiled=True).reshape(x.shape)


def shards(
    points,
    decay_one,
    decay_two,
    block_target,
    w_qkv_one,
    w_out_one,
    w_up,
    w_down,
    w_qkv_two,
    w_out_two,
):
    joined = jnp.concatenate([w_up.T, w_down], axis=1)
    spread = jnp.broadcast_to(joined[None], (8, 16, 2 * D))
    column = lax.all_to_all(spread, "seq_0", split_axis=0, concat_axis=0, tiled=True)
    column = column.reshape(128, 2 * D)
    position = lax.axis_index(SEQ)
    core = lax.axis_index("seq_2")
    limits = CAP * (position - core + iota((3, 1), 0))
    starts = jnp.sum((block_target[None, :] < limits).astype(jnp.int32), axis=1)
    meta = jnp.concatenate([starts, jnp.stack([core]).astype(jnp.int32)])
    own = lax.dynamic_slice_in_dim(block_target, position * 16, 16)
    chips = jnp.repeat(own // (2 * CAP), BR)[None, :]

    normed, keys_values, sent = kernel_call(
        front,
        [((128, D), BF16), ((128, 2 * D), BF16), ((512, 128), BF16)],
        points,
        w_qkv_one,
        decay_one,
        loose=(0, 1, 2),
    )
    column, sent = lax.optimization_barrier((column, sent))
    weights = lax.all_gather(column, ROW, axis=0, tiled=True)
    received = whole(sent, SEQ, 128)
    own_rows = kernel_call(
        inner,
        [((128, D), BF16), ((128, D), F32), ((128, HEADS), F32)],
        normed,
        w_qkv_one,
        keys_values,
        decay_one,
        loose=(0, 2, 3),
        outside=(1,),
    )
    entering = whole(kernel_call(prefix, [((256, 128), BF16)], received), SEQ, 128)
    outgoing = kernel_call(
        middle, [((512, D), BF16)], chips, points, *own_rows, entering, w_out_one
    )
    arrived = whole(outgoing, CHIPS, 64)
    outgoing = kernel_call(across, [((256, D), BF16)], meta, arrived, scalars=1)
    arrived = whole(outgoing, "seq_2", 2)
    placed, normed, keys_values, decay, sent = kernel_call(
        second,
        [
            ((256, D), BF16),
            ((256, D), BF16),
            ((256, 2 * D), BF16),
            ((HEADS, 256), F32),
            ((512, 128), BF16),
        ],
        meta,
        arrived,
        w_qkv_two,
        decay_two,
        weights,
        scalars=1,
        streamed=(4,),
        scratch=(
            pltpu.VMEM((4 * D, D), BF16),
            pltpu.VMEM((4 * D, D), BF16),
            pltpu.SemaphoreType.DMA((2,)),
        ),
    )
    received = whole(sent, SEQ, 128)
    own_rows = kernel_call(
        inner,
        [((256, D), BF16), ((256, D), F32), ((256, HEADS), F32)],
        normed,
        w_qkv_two,
        keys_values,
        decay,
        loose=(0, 2, 3),
        outside=(1,),
    )
    entering = whole(kernel_call(prefix, [((256, 128), BF16)], received), SEQ, 128)
    return kernel_call(last, [((256, D), BF16)], placed, *own_rows, entering, w_out_two)


def solution(mesh):
    split = Mesh(
        mesh.devices.reshape(8, 8, 2, mesh.shape["rep"]), ("seq_0", "seq_1", "seq_2", "rep")
    )
    placed = (
        P(REP_SEQ, None),
        P(None, REP_SEQ),
        P(None, REP_SEQ),
        P("rep"),
        P(),
        P(),
        P(None, SEQ),
        P(SEQ, None),
        P(),
        P(),
    )
    return jax.shard_map(
        shards, mesh=split, in_specs=placed, out_specs=P(REP_SEQ, None), check_vma=False
    )
```

```python
import jax
import jax.numpy as jnp
from jax import lax
from jax.experimental import pallas as pl
from jax.experimental.pallas import tpu as pltpu
from jax.sharding import Mesh
from jax.sharding import PartitionSpec as P

D = 512
HEADS = 8
HEAD_DIM = 64
PAIRS = HEADS // 2
BR = 8
CAP = 32
SEQ = ("seq_0", "seq_1", "seq_2", "seq_3")
GROUPS = ("seq_0", "seq_1")
INSIDE = ("seq_2", "seq_3")
ROW = ("seq_1", "seq_2", "seq_3")
REP_SEQ = ("rep",) + SEQ
EPS = 1e-05
F32 = jnp.float32
BF16 = jnp.bfloat16
DIRECT = False

NN = (((1,), (0,)), ((), ()))
NT = (((1,), (1,)), ((), ()))
TN = (((0,), (0,)), ((), ()))


def dot(a, b, dims=NN):
    return lax.dot_general(a, b, dims, preferred_element_type=F32)


def iota(shape, dim):
    return lax.broadcasted_iota(jnp.int32, shape, dim)


def ones_where(cond):
    return jnp.where(cond, 1.0, 0.0).astype(BF16)


def halves(x):
    high = x.astype(BF16)
    return high, (x - high.astype(F32)).astype(BF16)


def thirds(x):
    high, rest = x.astype(BF16), x - x.astype(BF16).astype(F32)
    middle, low = halves(rest)
    return high, middle, low


def rms_rows(wide):
    return wide * lax.rsqrt(jnp.mean(wide * wide, axis=-1, keepdims=True) + EPS)


def running_sums(decay):
    rows = decay.shape[1]
    parts = thirds(decay)
    upto = ones_where(iota((rows, rows), 0) >= iota((rows, rows), 1))
    by_head = sum(dot(part, upto, NT) for part in parts)
    by_row = sum(dot(upto, part, NT) for part in parts)
    return by_head, by_row


def pair_lanes(columns, pair):
    rows = columns.shape[0]
    first = iota((rows, 2 * HEAD_DIM), 1) < HEAD_DIM
    return jnp.where(
        first, columns[:, 2 * pair : 2 * pair + 1], columns[:, 2 * pair + 1 : 2 * pair + 2]
    )


def pack_state(keys_values, by_row, more=None):
    rows = keys_values.shape[0]
    total = by_row[rows - 1 : rows]
    weight = jnp.exp(total - by_row)
    lane = iota((HEAD_DIM, 128), 1)
    each = 4 if more is None else 12
    place, column = iota((32 * each, 128), 0), iota((32 * each, 128), 1)
    device = place >> 2 if more is None else (place * 43691) >> 19
    kind = place - each * device
    spread = ones_where((kind < 2) & (column == 2 * device + kind))[:, :HEAD_DIM]
    if more is not None:
        chosen = (kind >= 4) & (column == (kind - 4) * 16 + (device & 15))
        more = dot(ones_where(chosen), more)
    packed = []
    for p in range(PAIRS):
        keys = keys_values[:, 128 * p : 128 * (p + 1)].astype(F32) * pair_lanes(weight, p)
        values = keys_values[:, D + 128 * p : D + 128 * (p + 1)]
        high, low = halves(keys)
        both = dot(high, values, TN) + dot(low, values, TN)
        state = jnp.where(lane < HEAD_DIM, both[:HEAD_DIM], both[HEAD_DIM:]).astype(BF16)
        high, low = halves(pair_lanes(total, p))
        piece = dot(spread, state)
        piece = jnp.where(kind == 2, high.astype(F32), piece)
        piece = jnp.where(kind == 3, low.astype(F32), piece)
        if more is not None:
            piece = jnp.where(kind >= 4, more, piece)
        packed.append(piece.astype(BF16))
    return jnp.concatenate(packed, axis=0)


def front(points, weight, decay, up, down):
    normed = rms_rows(points[...].astype(F32)).astype(BF16)
    keys_values = dot(normed, weight[:, D:]).astype(BF16)
    by_row = running_sums(decay[...])[1]
    more = [part[:, 128 * k : 128 * (k + 1)] for part in (up, down) for k in range(4)]
    more = jnp.concatenate(more, axis=0)
    return normed, keys_values, pack_state(keys_values, by_row, more)


def prefix(received):
    each = received.shape[0] // 128
    block = (16 * each, 16 * each)
    kind, device = iota(block, 0) >> 4, iota(block, 0) & 15
    sort = ones_where(iota(block, 1) == each * device + kind)
    blocks = [
        dot(sort, received[16 * each * g : 16 * each * (g + 1), :]).astype(BF16) for g in range(8)
    ]

    def rows_of(kind):
        return jnp.concatenate([block[16 * kind : 16 * (kind + 1)] for block in blocks], axis=0)

    states = [rows_of(j) for j in range(2)]
    totals = [rows_of(2 + j).astype(F32) for j in range(2)]
    square = (128, 128)
    earlier = iota(square, 1) < iota(square, 0)
    before = ones_where(earlier)
    later = iota(square, 0) > iota(square, 1)
    outs = []
    for half in range(2):
        gap = sum(
            dot(
                before,
                jnp.where(later, part[:, half * HEAD_DIM : half * HEAD_DIM + 1], 0.0).astype(BF16),
            )
            for part in totals
        )
        high, low = halves(jnp.where(earlier, jnp.exp(gap), 0.0))
        outs.append([dot(high, state) + dot(low, state) for state in states])
    lane = iota(square, 1) < HEAD_DIM
    back = iota((256, 128), 0) - 2 * iota((256, 128), 1)
    summed = sum(
        dot(ones_where(back == j), jnp.where(lane, outs[0][j], outs[1][j]).astype(BF16))
        for j in range(2)
    ).astype(BF16)
    if each == 4:
        return summed
    return summed, jnp.concatenate([rows_of(kind) for kind in range(4, each)], axis=1)


def inner(normed, weight, keys_values, decay):
    by_head, by_row = running_sums(decay[...])
    queries = (dot(normed[...], weight[:, :D]) * HEAD_DIM ** (-0.5)).astype(BF16)
    rows = queries.shape[0]
    causal = iota((rows, rows), 0) >= iota((rows, rows), 1)
    lanes = iota((1, 128), 1)
    sides = (ones_where(lanes < HEAD_DIM), ones_where(lanes >= HEAD_DIM))
    first = iota((rows, 128), 1) < HEAD_DIM
    summed = []
    for p in range(PAIRS):
        query = queries[:, 128 * p : 128 * (p + 1)]
        keys = keys_values[:, 128 * p : 128 * (p + 1)]
        values = keys_values[:, D + 128 * p : D + 128 * (p + 1)]
        both = []
        for side in range(2):
            h = 2 * p + side
            scores = dot(query * sides[side], keys, NT)
            gap = by_row[:, h : h + 1] - by_head[h : h + 1, :]
            weighted = scores * jnp.exp(jnp.where(causal, gap, -1e30))
            both.append(dot(weighted.astype(BF16), values))
        summed.append(jnp.where(first, both[0], both[1]))
    return queries, jnp.concatenate(summed, axis=1), jnp.exp(by_row)


def attended(queries, summed, grown, entering):
    lanes = iota((1, 128), 1)
    sides = (ones_where(lanes < HEAD_DIM), ones_where(lanes >= HEAD_DIM))
    same = ones_where(iota((128, 128), 0) // HEAD_DIM == iota((128, 128), 1) // HEAD_DIM)
    outs = []
    for p in range(PAIRS):
        state = entering[HEAD_DIM * p : HEAD_DIM * (p + 1), :]
        state = jnp.concatenate([state * sides[0], state * sides[1]], axis=0)
        carried = dot(queries[:, 128 * p : 128 * (p + 1)], state) * pair_lanes(grown[...], p)
        number = summed[:, 128 * p : 128 * (p + 1)] + carried
        high, low = halves(number * number)
        mean = (dot(high, same) + dot(low, same)) * (1.0 / HEAD_DIM)
        outs.append((number * lax.rsqrt(mean + EPS)).astype(BF16))
    return jnp.concatenate(outs, axis=1)


def middle(fours, points, queries, summed, grown, entering, w_out):
    mixed = dot(attended(queries, summed, grown, entering), w_out[...])
    first = (points[...].astype(F32) + mixed).astype(BF16)
    shape = (256, 128)
    place, column = iota(shape, 0), iota(shape, 1)
    chosen = (place // BR == fours[...]) & ((place & 7) == (column & 7))
    return dot(ones_where(chosen), first).astype(BF16)


def across(meta, arrived):
    shape = (256, 256)
    place, column = iota(shape, 0), iota(shape, 1)
    begin = sum(jnp.where(place // 64 == k, meta[k], 0) for k in range(4))
    end = sum(jnp.where(place // 64 == k, meta[k + 1], 0) for k in range(4))
    where = begin + ((meta[5] - begin) & 3) + 4 * ((place // BR) & 7)
    held = (where & 127) >> 2
    chosen = (where < end) & (column == held * BR + (place & 7))
    return dot(ones_where(chosen), arrived[...]).astype(BF16)


def second(meta, arrived, w_qkv, decay, weights, up=None, down=None, copies=None):
    pieces = []
    if up is None:
        up, down = weights[:, :D], weights[:, D:]
    else:
        for k, buffer in enumerate((up, down)):
            pieces.append(
                pltpu.make_async_copy(weights.at[:, pl.ds(k * D, D)], buffer, copies.at[k])
            )
            pieces[k].start()
    shape = (256, 256)
    place, column = iota(shape, 0), iota(shape, 1)
    begin = meta[meta[5]]
    used = meta[meta[5] + 1] - begin
    slot = place // BR
    held = ((begin + slot) & 3) * 8 + slot // 4
    chosen = (slot < used) & (column == held * BR + (place & 7))
    kept = jnp.where(iota(decay.shape, 1) < BR * used, decay[...], 0.0)
    by_row = running_sums(kept)[1]
    first = dot(ones_where(chosen), arrived[...])
    normed = rms_rows(first).astype(BF16)
    if pieces:
        pieces[0].wait()
    hidden = jax.nn.gelu(dot(normed, up[...], NT), approximate=True).astype(BF16)
    if pieces:
        pieces[1].wait()
    placed = (first + dot(hidden, down[...])).astype(BF16)
    normed = rms_rows(placed.astype(F32)).astype(BF16)
    keys_values = dot(normed, w_qkv[:, D:]).astype(BF16)
    return placed, normed, keys_values, kept, pack_state(keys_values, by_row)


def last(placed, queries, summed, grown, entering, w_out):
    mixed = dot(attended(queries, summed, grown, entering), w_out[...])
    return (placed[...].astype(F32) + mixed).astype(BF16)


def kernel_call(function, outs, *args, scalars=0, loose=(), outside=(), streamed=(), scratch=()):
    if DIRECT:
        return function(*args)
    count = len(args)

    def body(*refs):
        results = function(*refs[:count], *refs[count + len(outs) :])
        if len(outs) == 1:
            results = (results,)
        for ref, value in zip(refs[count:], results):
            ref[...] = value

    def spec(k):
        if k < scalars:
            return pl.BlockSpec(memory_space=pltpu.SMEM)
        return pl.BlockSpec(memory_space=pltpu.HBM if k in streamed else pltpu.VMEM)

    args = [
        arg
        if k < scalars or k in loose
        else pltpu.with_memory_space_constraint(
            arg, pltpu.HBM if k in streamed + outside else pltpu.VMEM
        )
        for k, arg in enumerate(args)
    ]
    result = pl.pallas_call(
        body,
        compiler_params=pltpu.CompilerParams(vmem_limit_bytes=32 << 20),
        out_shape=[jax.ShapeDtypeStruct(shape, kind) for shape, kind in outs],
        in_specs=[spec(k) for k in range(count)],
        out_specs=[pl.BlockSpec(memory_space=pltpu.VMEM)] * len(outs),
        scratch_shapes=list(scratch),
        name=function.__name__,
    )(*args)
    return result[0] if len(outs) == 1 else result


def whole(x, axes, pieces):
    split = x.reshape(pieces, x.shape[0] // pieces, x.shape[1])
    return lax.all_to_all(split, axes, split_axis=0, concat_axis=0, tiled=True).reshape(x.shape)


def shards(
    points,
    decay_one,
    decay_two,
    block_target,
    w_qkv_one,
    w_out_one,
    w_up,
    w_down,
    w_qkv_two,
    w_out_two,
):
    position = lax.axis_index(SEQ)
    member = position & 3
    limits = CAP * (position - member + iota((5, 1), 0))
    starts = jnp.sum((block_target[None, :] < limits).astype(jnp.int32), axis=1)
    meta = jnp.concatenate([starts, member[None].astype(jnp.int32)])
    own = lax.dynamic_slice_in_dim(block_target, position * 16, 16)
    fours = jnp.repeat(own // (4 * CAP), BR)[None, :]

    normed, keys_values, sent = kernel_call(
        front,
        [((128, D), BF16), ((128, 2 * D), BF16), ((1536, 128), BF16)],
        points,
        w_qkv_one,
        decay_one,
        w_up.T,
        w_down,
        outside=(0, 1, 2, 3, 4),
    )
    received = lax.all_to_all(
        sent.reshape(384, 4, 128), SEQ, split_axis=0, concat_axis=0, tiled=True
    ).reshape(1536, 128)
    summed, column = kernel_call(
        prefix, [((256, 128), BF16), ((128, 2 * D), BF16)], received
    )
    weights = lax.all_gather(column, ROW, axis=0, tiled=True)
    own_rows = kernel_call(
        inner,
        [((128, D), BF16), ((128, D), F32), ((128, HEADS), F32)],
        normed,
        w_qkv_one,
        keys_values,
        decay_one,
        loose=(0, 2, 3),
        outside=(1,),
    )
    entering = whole(summed, SEQ, 128)
    outgoing = kernel_call(
        middle, [((256, D), BF16)], fours, points, *own_rows, entering, w_out_one
    )
    arrived = whole(outgoing, GROUPS, 32)
    outgoing = kernel_call(across, [((256, D), BF16)], meta, arrived, scalars=1)
    arrived = whole(outgoing, INSIDE, 4)
    placed, normed, keys_values, decay, sent = kernel_call(
        second,
        [
            ((256, D), BF16),
            ((256, D), BF16),
            ((256, 2 * D), BF16),
            ((HEADS, 256), F32),
            ((512, 128), BF16),
        ],
        meta,
        arrived,
        w_qkv_two,
        decay_two,
        weights,
        scalars=1,
        streamed=(4,),
        scratch=(
            pltpu.VMEM((4 * D, D), BF16),
            pltpu.VMEM((4 * D, D), BF16),
            pltpu.SemaphoreType.DMA((2,)),
        ),
    )
    received = whole(sent, SEQ, 128)
    own_rows = kernel_call(
        inner,
        [((256, D), BF16), ((256, D), F32), ((256, HEADS), F32)],
        normed,
        w_qkv_two,
        keys_values,
        decay,
        loose=(0, 2, 3),
        outside=(1,),
    )
    entering = whole(kernel_call(prefix, [((256, 128), BF16)], received), SEQ, 128)
    return kernel_call(last, [((256, D), BF16)], placed, *own_rows, entering, w_out_two)


def solution(mesh):
    split = Mesh(
        mesh.devices.reshape(8, 4, 2, 2, mesh.shape["rep"]), SEQ + ("rep",)
    )
    placed = (
        P(REP_SEQ, None),
        P(None, REP_SEQ),
        P(None, REP_SEQ),
        P("rep"),
        P(),
        P(),
        P(None, SEQ),
        P(SEQ, None),
        P(),
        P(),
    )
    return jax.shard_map(
        shards, mesh=split, in_specs=placed, out_specs=P(REP_SEQ, None), check_vma=False
    )
```

```python
import jax
import jax.numpy as jnp
from jax import lax
from jax.experimental import pallas as pl
from jax.experimental.pallas import tpu as pltpu
from jax.sharding import Mesh
from jax.sharding import PartitionSpec as P

D = 512
HEADS = 8
HEAD_DIM = 64
PAIRS = HEADS // 2
BR = 8
CAP = 32
SEQ = ("seq_0", "seq_1", "seq_2", "seq_3")
GROUPS = ("seq_0", "seq_1")
INSIDE = ("seq_2", "seq_3")
ROW = ("seq_1", "seq_2", "seq_3")
REP_SEQ = ("rep",) + SEQ
EPS = 1e-05
F32 = jnp.float32
BF16 = jnp.bfloat16
DIRECT = False

NN = (((1,), (0,)), ((), ()))
NT = (((1,), (1,)), ((), ()))
TN = (((0,), (0,)), ((), ()))


def dot(a, b, dims=NN):
    return lax.dot_general(a, b, dims, preferred_element_type=F32)


def iota(shape, dim):
    return lax.broadcasted_iota(jnp.int32, shape, dim)


def ones_where(cond):
    return jnp.where(cond, 1.0, 0.0).astype(BF16)


def halves(x):
    high = x.astype(BF16)
    return high, (x - high.astype(F32)).astype(BF16)


def thirds(x):
    high, rest = x.astype(BF16), x - x.astype(BF16).astype(F32)
    middle, low = halves(rest)
    return high, middle, low


def rms_rows(wide):
    return wide * lax.rsqrt(jnp.mean(wide * wide, axis=-1, keepdims=True) + EPS)


def running_sums(decay):
    rows = decay.shape[1]
    parts = thirds(decay)
    upto = ones_where(iota((rows, rows), 0) >= iota((rows, rows), 1))
    by_head = sum(dot(part, upto, NT) for part in parts)
    by_row = sum(dot(upto, part, NT) for part in parts)
    return by_head, by_row


def pair_lanes(columns, pair):
    rows = columns.shape[0]
    first = iota((rows, 2 * HEAD_DIM), 1) < HEAD_DIM
    return jnp.where(
        first, columns[:, 2 * pair : 2 * pair + 1], columns[:, 2 * pair + 1 : 2 * pair + 2]
    )


def own_state(keys_values, by_row):
    rows = keys_values.shape[0]
    weight = jnp.exp(by_row[rows - 1 : rows] - by_row)
    lane = iota((HEAD_DIM, 128), 1)
    states = []
    for p in range(PAIRS):
        keys = keys_values[:, 128 * p : 128 * (p + 1)].astype(F32) * pair_lanes(weight, p)
        values = keys_values[:, D + 128 * p : D + 128 * (p + 1)]
        both = dot(keys.astype(BF16), values, TN)
        states.append(jnp.where(lane < HEAD_DIM, both[:HEAD_DIM], both[HEAD_DIM:]).astype(BF16))
    return states


def pack(states, totals, more):
    place, column = iota((384, 128), 0), iota((384, 128), 1)
    device = (place * 43691) >> 19
    kind = place - 12 * device
    spread = ones_where((kind < 2) & (column == 2 * device + kind))[:, :HEAD_DIM]
    chosen = (kind >= 4) & (column == (kind - 4) * 16 + (device & 15))
    more = dot(ones_where(chosen), more)
    even = (iota((1, 128), 1) & 1) == 0
    packed = []
    for p in range(PAIRS):
        total = jnp.where(even, pair_lanes(totals[0], p), pair_lanes(totals[1], p))
        high, low = halves(total)
        piece = dot(spread, states[p]) + more
        piece = jnp.where(kind == 2, high.astype(F32), piece)
        piece = jnp.where(kind == 3, low.astype(F32), piece)
        packed.append(piece.astype(BF16))
    return jnp.concatenate(packed, axis=0)


def front(here, points, weight, decay, up, down, later, target):
    normed = rms_rows(points[...].astype(F32)).astype(BF16)
    keys_values = dot(normed, weight[:, D:]).astype(BF16)
    by_row = running_sums(decay[...])[1]
    used = jnp.where((target[...] >> 5) == here[0], 1.0, 0.0)
    used = jnp.sum(jnp.sum(used, axis=0, keepdims=True), axis=1, keepdims=True)
    kept = jnp.where(iota(later.shape, 1).astype(F32) < BR * used, later[...], 0.0)
    ones = ones_where(iota(later.shape, 0) >= 0)
    second_total = sum(dot(ones, part, NT) for part in thirds(kept))[:1]
    totals = (by_row[by_row.shape[0] - 1 :], second_total)
    more = [part[:, 128 * k : 128 * (k + 1)] for part in (up, down) for k in range(4)]
    more = jnp.concatenate(more, axis=0)
    return normed, keys_values, pack(own_state(keys_values, by_row), totals, more)


def sort(received):
    block = (192, 192)
    kind, device = iota(block, 0) >> 4, iota(block, 0) & 15
    order = ones_where(iota(block, 1) == 12 * device + kind)
    blocks = [dot(order, received[192 * g : 192 * (g + 1), :]).astype(BF16) for g in range(8)]

    def rows_of(kind):
        return jnp.concatenate([block[16 * kind : 16 * (kind + 1)] for block in blocks], axis=0)

    return (
        jnp.concatenate([rows_of(kind) for kind in range(4)], axis=0),
        jnp.concatenate([rows_of(kind) for kind in range(4, 12)], axis=1),
    )


def device_weights(heads, layer):
    square = (128, 128)
    earlier = iota(square, 1) < iota(square, 0)
    later = iota(square, 0) > iota(square, 1)
    before = ones_where(earlier)
    before = jnp.concatenate([before, before], axis=1)
    weights = []
    for half in range(2):
        at = half * HEAD_DIM + layer
        parts = [
            jnp.where(later, heads[128 * k : 128 * (k + 1), at : at + 1].astype(F32), 0.0)
            for k in (2, 3)
        ]
        gap = dot(before, jnp.concatenate(parts, axis=0).astype(BF16))
        high, low = halves(jnp.where(earlier, jnp.exp(gap), 0.0))
        weights.append(jnp.concatenate([high, low], axis=1))
    return weights


def gather_earlier(weights, states):
    both = jnp.concatenate([states, states], axis=0)
    outs = [dot(weight, both) for weight in weights]
    lane = iota(outs[0].shape, 1) & 127
    out = jnp.where(lane < HEAD_DIM, outs[0], outs[1]).astype(BF16)
    out = jnp.concatenate([out[:, :128], out[:, 128:]], axis=0)
    place, column = iota((256, 256), 0), iota((256, 256), 1)
    back = ones_where(column == (place & 1) * 128 + (place >> 1))
    return dot(back, out).astype(BF16)


def prefix(heads):
    states = jnp.concatenate([heads[:128, :], heads[128:256, :]], axis=1)
    return gather_earlier(device_weights(heads, 0), states)


def later_weights(heads):
    return jnp.concatenate(device_weights(heads, 1), axis=0)


def later_prefix(received, weights):
    place, column = iota((256, 256), 0), iota((256, 256), 1)
    order = ones_where(column == 2 * (place & 127) + (place >> 7))
    rows = dot(order, received[...]).astype(BF16)
    states = jnp.concatenate([rows[:128], rows[128:]], axis=1)
    return gather_earlier([weights[:128, :], weights[128:, :]], states)


def inner(normed, weight, keys_values, decay):
    by_head, by_row = running_sums(decay[...])
    queries = (dot(normed[...], weight[:, :D]) * HEAD_DIM ** (-0.5)).astype(BF16)
    rows = queries.shape[0]
    causal = iota((rows, rows), 0) >= iota((rows, rows), 1)
    lanes = iota((1, 128), 1)
    sides = (ones_where(lanes < HEAD_DIM), ones_where(lanes >= HEAD_DIM))
    first = iota((rows, 128), 1) < HEAD_DIM
    summed = []
    for p in range(PAIRS):
        query = queries[:, 128 * p : 128 * (p + 1)]
        keys = keys_values[:, 128 * p : 128 * (p + 1)]
        values = keys_values[:, D + 128 * p : D + 128 * (p + 1)]
        both = []
        for side in range(2):
            h = 2 * p + side
            scores = dot(query * sides[side], keys, NT)
            gap = by_row[:, h : h + 1] - by_head[h : h + 1, :]
            weighted = scores * jnp.exp(jnp.where(causal, gap, -1e30))
            both.append(dot(weighted.astype(BF16), values))
        summed.append(jnp.where(first, both[0], both[1]))
    return queries, jnp.concatenate(summed, axis=1), jnp.exp(by_row)


def attended(queries, summed, grown, entering):
    lanes = iota((1, 128), 1)
    sides = (ones_where(lanes < HEAD_DIM), ones_where(lanes >= HEAD_DIM))
    same = ones_where(iota((128, 128), 0) // HEAD_DIM == iota((128, 128), 1) // HEAD_DIM)
    outs = []
    for p in range(PAIRS):
        state = entering[HEAD_DIM * p : HEAD_DIM * (p + 1), :]
        state = jnp.concatenate([state * sides[0], state * sides[1]], axis=0)
        carried = dot(queries[:, 128 * p : 128 * (p + 1)], state) * pair_lanes(grown[...], p)
        number = summed[:, 128 * p : 128 * (p + 1)] + carried
        high, low = halves(number * number)
        mean = (dot(high, same) + dot(low, same)) * (1.0 / HEAD_DIM)
        outs.append((number * lax.rsqrt(mean + EPS)).astype(BF16))
    return jnp.concatenate(outs, axis=1)


def middle(fours, points, queries, summed, grown, entering, w_out):
    mixed = dot(attended(queries, summed, grown, entering), w_out[...])
    first = (points[...].astype(F32) + mixed).astype(BF16)
    shape = (256, 128)
    place, column = iota(shape, 0), iota(shape, 1)
    chosen = (place // BR == fours[...]) & ((place & 7) == (column & 7))
    return dot(ones_where(chosen), first).astype(BF16)


def across(meta, arrived):
    shape = (256, 256)
    place, column = iota(shape, 0), iota(shape, 1)
    begin = sum(jnp.where(place // 64 == k, meta[k], 0) for k in range(4))
    end = sum(jnp.where(place // 64 == k, meta[k + 1], 0) for k in range(4))
    where = begin + ((meta[5] - begin) & 3) + 4 * ((place // BR) & 7)
    held = (where & 127) >> 2
    chosen = (where < end) & (column == held * BR + (place & 7))
    return dot(ones_where(chosen), arrived[...]).astype(BF16)


def second(meta, arrived, w_qkv, decay, weights, up=None, down=None, copies=None):
    pieces = []
    if up is None:
        up, down = weights[:, :D], weights[:, D:]
    else:
        for k, buffer in enumerate((up, down)):
            pieces.append(
                pltpu.make_async_copy(weights.at[:, pl.ds(k * D, D)], buffer, copies.at[k])
            )
            pieces[k].start()
    shape = (256, 256)
    place, column = iota(shape, 0), iota(shape, 1)
    begin = meta[meta[5]]
    used = meta[meta[5] + 1] - begin
    slot = place // BR
    held = ((begin + slot) & 3) * 8 + slot // 4
    chosen = (slot < used) & (column == held * BR + (place & 7))
    kept = jnp.where(iota(decay.shape, 1) < BR * used, decay[...], 0.0)
    by_row = running_sums(kept)[1]
    first = dot(ones_where(chosen), arrived[...])
    normed = rms_rows(first).astype(BF16)
    if pieces:
        pieces[0].wait()
    hidden = jax.nn.gelu(dot(normed, up[...], NT), approximate=True).astype(BF16)
    if pieces:
        pieces[1].wait()
    placed = (first + dot(hidden, down[...])).astype(BF16)
    normed = rms_rows(placed.astype(F32)).astype(BF16)
    keys_values = dot(normed, w_qkv[:, D:]).astype(BF16)
    state = jnp.concatenate(own_state(keys_values, by_row), axis=0)
    return placed, normed, keys_values, kept, state


def last(placed, queries, summed, grown, entering, w_out):
    mixed = dot(attended(queries, summed, grown, entering), w_out[...])
    return (placed[...].astype(F32) + mixed).astype(BF16)


def kernel_call(function, outs, *args, scalars=0, loose=(), outside=(), streamed=(), scratch=()):
    if DIRECT:
        return function(*args)
    count = len(args)

    def body(*refs):
        results = function(*refs[:count], *refs[count + len(outs) :])
        if len(outs) == 1:
            results = (results,)
        for ref, value in zip(refs[count:], results):
            ref[...] = value

    def spec(k):
        if k < scalars:
            return pl.BlockSpec(memory_space=pltpu.SMEM)
        return pl.BlockSpec(memory_space=pltpu.HBM if k in streamed else pltpu.VMEM)

    args = [
        arg
        if k < scalars or k in loose
        else pltpu.with_memory_space_constraint(
            arg, pltpu.HBM if k in streamed + outside else pltpu.VMEM
        )
        for k, arg in enumerate(args)
    ]
    result = pl.pallas_call(
        body,
        compiler_params=pltpu.CompilerParams(vmem_limit_bytes=32 << 20),
        out_shape=[jax.ShapeDtypeStruct(shape, kind) for shape, kind in outs],
        in_specs=[spec(k) for k in range(count)],
        out_specs=[pl.BlockSpec(memory_space=pltpu.VMEM)] * len(outs),
        scratch_shapes=list(scratch),
        name=function.__name__,
    )(*args)
    return result[0] if len(outs) == 1 else result


def whole(x, axes, pieces):
    split = x.reshape(pieces, x.shape[0] // pieces, x.shape[1])
    return lax.all_to_all(split, axes, split_axis=0, concat_axis=0, tiled=True).reshape(x.shape)


def shards(
    points,
    decay_one,
    decay_two,
    block_target,
    w_qkv_one,
    w_out_one,
    w_up,
    w_down,
    w_qkv_two,
    w_out_two,
):
    position = lax.axis_index(SEQ)
    member = position & 3
    limits = CAP * (position - member + iota((5, 1), 0))
    starts = jnp.sum((block_target[None, :] < limits).astype(jnp.int32), axis=1)
    meta = jnp.concatenate([starts, member[None].astype(jnp.int32)])
    own = lax.dynamic_slice_in_dim(block_target, position * 16, 16)
    fours = jnp.repeat(own // (4 * CAP), BR)[None, :]

    normed, keys_values, sent = kernel_call(
        front,
        [((128, D), BF16), ((128, 2 * D), BF16), ((1536, 128), BF16)],
        position[None].astype(jnp.int32),
        points,
        w_qkv_one,
        decay_one,
        w_up.T,
        w_down,
        decay_two,
        block_target.reshape(16, 128),
        scalars=1,
        outside=(1, 2, 3, 4, 5, 6, 7),
    )
    received = lax.all_to_all(
        sent.reshape(384, 4, 128), SEQ, split_axis=0, concat_axis=0, tiled=True
    ).reshape(1536, 128)
    heads, column = kernel_call(sort, [((512, 128), BF16), ((128, 2 * D), BF16)], received)
    weights = lax.all_gather(column, ROW, axis=0, tiled=True)
    summed = kernel_call(prefix, [((256, 128), BF16)], heads)
    device_weight = kernel_call(later_weights, [((256, 256), BF16)], heads)
    own_rows = kernel_call(
        inner,
        [((128, D), BF16), ((128, D), F32), ((128, HEADS), F32)],
        normed,
        w_qkv_one,
        keys_values,
        decay_one,
        loose=(0, 2, 3),
        outside=(1,),
    )
    entering = whole(summed, SEQ, 128)
    outgoing = kernel_call(
        middle, [((256, D), BF16)], fours, points, *own_rows, entering, w_out_one
    )
    arrived = whole(outgoing, GROUPS, 32)
    outgoing = kernel_call(across, [((256, D), BF16)], meta, arrived, scalars=1)
    arrived = whole(outgoing, INSIDE, 4)
    placed, normed, keys_values, decay, sent = kernel_call(
        second,
        [
            ((256, D), BF16),
            ((256, D), BF16),
            ((256, 2 * D), BF16),
            ((HEADS, 256), F32),
            ((256, 128), BF16),
        ],
        meta,
        arrived,
        w_qkv_two,
        decay_two,
        weights,
        scalars=1,
        streamed=(4,),
        scratch=(
            pltpu.VMEM((4 * D, D), BF16),
            pltpu.VMEM((4 * D, D), BF16),
            pltpu.SemaphoreType.DMA((2,)),
        ),
    )
    received = whole(sent, SEQ, 128)
    own_rows = kernel_call(
        inner,
        [((256, D), BF16), ((256, D), F32), ((256, HEADS), F32)],
        normed,
        w_qkv_two,
        keys_values,
        decay,
        loose=(0, 2, 3),
        outside=(1,),
    )
    summed = kernel_call(later_prefix, [((256, 128), BF16)], received, device_weight)
    entering = whole(summed, SEQ, 128)
    return kernel_call(last, [((256, D), BF16)], placed, *own_rows, entering, w_out_two)


def solution(mesh):
    split = Mesh(
        mesh.devices.reshape(8, 4, 2, 2, mesh.shape["rep"]), SEQ + ("rep",)
    )
    placed = (
        P(REP_SEQ, None),
        P(None, REP_SEQ),
        P(None, REP_SEQ),
        P("rep"),
        P(),
        P(),
        P(None, SEQ),
        P(SEQ, None),
        P(),
        P(),
    )
    return jax.shard_map(
        shards, mesh=split, in_specs=placed, out_specs=P(REP_SEQ, None), check_vma=False
    )
```

```python
import math

import jax
import jax.numpy as jnp
from jax import lax
from jax.experimental import pallas as pl
from jax.experimental.pallas import tpu as pltpu
from jax.sharding import Mesh
from jax.sharding import PartitionSpec as P

D = 512
HEADS = 8
HEAD_DIM = 64
PAIRS = HEADS // 2
BR = 8
CAP = 32
SEQ = ("seq_0", "seq_1", "seq_2", "seq_3")
GROUPS = ("seq_0", "seq_1")
INSIDE = ("seq_2", "seq_3")
ROW = ("seq_1", "seq_2", "seq_3")
REP_SEQ = ("rep",) + SEQ
EPS = 1e-05
GELU = (2.0 / math.pi) ** 0.5
F32 = jnp.float32
BF16 = jnp.bfloat16
DIRECT = False

NN = (((1,), (0,)), ((), ()))
NT = (((1,), (1,)), ((), ()))
TN = (((0,), (0,)), ((), ()))


def dot(a, b, dims=NN):
    return lax.dot_general(a, b, dims, preferred_element_type=F32)


def iota(shape, dim):
    return lax.broadcasted_iota(jnp.int32, shape, dim)


def ones_where(cond):
    return jnp.where(cond, 1.0, 0.0).astype(BF16)


def halves(x):
    high = x.astype(BF16)
    return high, (x - high.astype(F32)).astype(BF16)


def thirds(x):
    high, rest = x.astype(BF16), x - x.astype(BF16).astype(F32)
    middle, low = halves(rest)
    return high, middle, low


def rms_rows(wide):
    return wide * lax.rsqrt(jnp.mean(wide * wide, axis=-1, keepdims=True) + EPS)


def running_sums(decay):
    rows = decay.shape[1]
    parts = thirds(decay)
    upto = ones_where(iota((rows, rows), 0) >= iota((rows, rows), 1))
    by_head = sum(dot(part, upto, NT) for part in parts)
    by_row = sum(dot(upto, part, NT) for part in parts)
    return by_head, by_row


def pair_lanes(columns, pair):
    rows = columns.shape[0]
    first = iota((rows, 2 * HEAD_DIM), 1) < HEAD_DIM
    return jnp.where(
        first, columns[:, 2 * pair : 2 * pair + 1], columns[:, 2 * pair + 1 : 2 * pair + 2]
    )


def own_state(keys_values, by_row):
    rows = keys_values.shape[0]
    weight = jnp.exp(by_row[rows - 1 : rows] - by_row)
    lane = iota((HEAD_DIM, 128), 1)
    states = []
    for p in range(PAIRS):
        keys = keys_values[:, 128 * p : 128 * (p + 1)].astype(F32) * pair_lanes(weight, p)
        values = keys_values[:, D + 128 * p : D + 128 * (p + 1)]
        both = dot(keys.astype(BF16), values, TN)
        states.append(jnp.where(lane < HEAD_DIM, both[:HEAD_DIM], both[HEAD_DIM:]).astype(BF16))
    return states


def pack(states, totals, more):
    place, column = iota((384, 128), 0), iota((384, 128), 1)
    device = (place * 43691) >> 19
    kind = place - 12 * device
    spread = ones_where((kind < 2) & (column == 2 * device + kind))[:, :HEAD_DIM]
    chosen = (kind >= 4) & (column == (kind - 4) * 16 + (device & 15))
    more = dot(ones_where(chosen), more)
    even = (iota((1, 128), 1) & 1) == 0
    packed = []
    for p in range(PAIRS):
        total = jnp.where(even, pair_lanes(totals[0], p), pair_lanes(totals[1], p))
        high, low = halves(total)
        piece = dot(spread, states[p]) + more
        piece = jnp.where(kind == 2, high.astype(F32), piece)
        piece = jnp.where(kind == 3, low.astype(F32), piece)
        packed.append(piece.astype(BF16))
    return jnp.concatenate(packed, axis=0)


def front(here, points, weight, decay, up, down, later, target, buffer=None, copies=None):
    if buffer is not None:
        piece = pltpu.make_async_copy(weight.at[:, pl.ds(D, 2 * D)], buffer, copies.at[0])
        piece.start()
    normed = rms_rows(points[...].astype(F32)).astype(BF16)
    by_row = running_sums(decay[...])[1]
    used = jnp.where((target[...] >> 5) == here[0], 1.0, 0.0)
    used = jnp.sum(jnp.sum(used, axis=0, keepdims=True), axis=1, keepdims=True)
    kept = jnp.where(iota(later.shape, 1).astype(F32) < BR * used, later[...], 0.0)
    ones = ones_where(iota(later.shape, 0) >= 0)
    second_total = sum(dot(ones, part, NT) for part in thirds(kept))[:1]
    totals = (by_row[by_row.shape[0] - 1 :], second_total)
    more = [part[:, 128 * k : 128 * (k + 1)] for part in (up, down) for k in range(4)]
    more = jnp.concatenate(more, axis=0)
    if buffer is None:
        buffer = weight[:, D:]
    else:
        piece.wait()
    keys_values = dot(normed, buffer[...]).astype(BF16)
    return normed, keys_values, pack(own_state(keys_values, by_row), totals, more)


def sort(received):
    block = (192, 192)
    kind, device = iota(block, 0) >> 4, iota(block, 0) & 15
    order = ones_where(iota(block, 1) == 12 * device + kind)
    blocks = [dot(order, received[192 * g : 192 * (g + 1), :]).astype(BF16) for g in range(8)]

    def rows_of(kind):
        return jnp.concatenate([block[16 * kind : 16 * (kind + 1)] for block in blocks], axis=0)

    return (
        jnp.concatenate([rows_of(kind) for kind in range(4)], axis=0),
        jnp.concatenate([rows_of(kind) for kind in range(4, 12)], axis=1),
    )


def device_weights(heads, layer):
    square = (128, 128)
    earlier = iota(square, 1) < iota(square, 0)
    later = iota(square, 0) > iota(square, 1)
    before = ones_where(earlier)
    before = jnp.concatenate([before, before], axis=1)
    weights = []
    for half in range(2):
        at = half * HEAD_DIM + layer
        parts = [
            jnp.where(later, heads[128 * k : 128 * (k + 1), at : at + 1].astype(F32), 0.0)
            for k in (2, 3)
        ]
        gap = dot(before, jnp.concatenate(parts, axis=0).astype(BF16))
        high, low = halves(jnp.where(earlier, jnp.exp(gap), 0.0))
        weights.append(jnp.concatenate([high, low], axis=1))
    return weights


def gather_earlier(weights, states):
    both = jnp.concatenate([states, states], axis=0)
    outs = [dot(weight, both) for weight in weights]
    lane = iota(outs[0].shape, 1) & 127
    out = jnp.where(lane < HEAD_DIM, outs[0], outs[1]).astype(BF16)
    out = jnp.concatenate([out[:, :128], out[:, 128:]], axis=0)
    place, column = iota((256, 256), 0), iota((256, 256), 1)
    back = ones_where(column == (place & 1) * 128 + (place >> 1))
    return dot(back, out).astype(BF16)


def prefix(heads):
    states = jnp.concatenate([heads[:128, :], heads[128:256, :]], axis=1)
    return gather_earlier(device_weights(heads, 0), states)


def later_weights(heads):
    return jnp.concatenate(device_weights(heads, 1), axis=0)


def later_prefix(received, weights):
    place, column = iota((256, 256), 0), iota((256, 256), 1)
    order = ones_where(column == 2 * (place & 127) + (place >> 7))
    rows = dot(order, received[...]).astype(BF16)
    states = jnp.concatenate([rows[:128], rows[128:]], axis=1)
    return gather_earlier([weights[:128, :], weights[128:, :]], states)


def inner(normed, weight, keys_values, decay):
    by_head, by_row = running_sums(decay[...])
    queries = (dot(normed[...], weight[:, :D]) * HEAD_DIM ** (-0.5)).astype(BF16)
    rows = queries.shape[0]
    causal = iota((rows, rows), 0) >= iota((rows, rows), 1)
    lanes = iota((1, 128), 1)
    sides = (ones_where(lanes < HEAD_DIM), ones_where(lanes >= HEAD_DIM))
    first = iota((rows, 128), 1) < HEAD_DIM
    summed = []
    for p in range(PAIRS):
        query = queries[:, 128 * p : 128 * (p + 1)]
        keys = keys_values[:, 128 * p : 128 * (p + 1)]
        values = keys_values[:, D + 128 * p : D + 128 * (p + 1)]
        both = []
        for side in range(2):
            h = 2 * p + side
            scores = dot(query * sides[side], keys, NT)
            gap = by_row[:, h : h + 1] - by_head[h : h + 1, :]
            weighted = scores * jnp.exp(jnp.where(causal, gap, -1e30))
            both.append(dot(weighted.astype(BF16), values))
        summed.append(jnp.where(first, both[0], both[1]))
    grown = jnp.exp(by_row)
    carrying = [
        queries[:, 128 * p : 128 * (p + 1)].astype(F32) * pair_lanes(grown, p)
        for p in range(PAIRS)
    ]
    return jnp.concatenate(carrying, axis=1).astype(BF16), jnp.concatenate(summed, axis=1)


def attended(carrying, summed, entering):
    lanes = iota((1, 128), 1)
    sides = (ones_where(lanes < HEAD_DIM), ones_where(lanes >= HEAD_DIM))
    same = ones_where(iota((128, 128), 0) // HEAD_DIM == iota((128, 128), 1) // HEAD_DIM)
    outs = []
    for p in range(PAIRS):
        state = entering[HEAD_DIM * p : HEAD_DIM * (p + 1), :]
        state = jnp.concatenate([state * sides[0], state * sides[1]], axis=0)
        number = summed[:, 128 * p : 128 * (p + 1)]
        number = number + dot(carrying[:, 128 * p : 128 * (p + 1)], state)
        mean = dot((number * number).astype(BF16), same) * (1.0 / HEAD_DIM)
        outs.append((number * lax.rsqrt(mean + EPS)).astype(BF16))
    return jnp.concatenate(outs, axis=1)


def middle(fours, points, carrying, summed, entering, w_out):
    mixed = dot(attended(carrying, summed, entering), w_out[...])
    first = (points[...].astype(F32) + mixed).astype(BF16)
    shape = (256, 128)
    place, column = iota(shape, 0), iota(shape, 1)
    chosen = (place // BR == fours[...]) & ((place & 7) == (column & 7))
    return dot(ones_where(chosen), first).astype(BF16)


def across(meta, arrived):
    shape = (256, 256)
    place, column = iota(shape, 0), iota(shape, 1)
    begin = sum(jnp.where(place // 64 == k, meta[k], 0) for k in range(4))
    end = sum(jnp.where(place // 64 == k, meta[k + 1], 0) for k in range(4))
    where = begin + ((meta[5] - begin) & 3) + 4 * ((place // BR) & 7)
    held = (where & 127) >> 2
    chosen = (where < end) & (column == held * BR + (place & 7))
    return dot(ones_where(chosen), arrived[...]).astype(BF16)


def second(meta, arrived, w_qkv, decay, weights, up=None, down=None, copies=None):
    pieces = []
    if up is None:
        up, down = weights[:, :D], weights[:, D:]
    else:
        for k, buffer in enumerate((up, down)):
            pieces.append(
                pltpu.make_async_copy(weights.at[:, pl.ds(k * D, D)], buffer, copies.at[k])
            )
            pieces[k].start()
    shape = (256, 256)
    place, column = iota(shape, 0), iota(shape, 1)
    begin = meta[meta[5]]
    used = meta[meta[5] + 1] - begin
    slot = place // BR
    held = ((begin + slot) & 3) * 8 + slot // 4
    chosen = (slot < used) & (column == held * BR + (place & 7))
    kept = jnp.where(iota(decay.shape, 1) < BR * used, decay[...], 0.0)
    by_row = running_sums(kept)[1]
    first = dot(ones_where(chosen), arrived[...])
    normed = rms_rows(first).astype(BF16)
    if pieces:
        pieces[0].wait()
    raw = dot(normed, up[...], NT)
    bent = jnp.tanh(raw * (GELU + (GELU * 0.044715) * (raw * raw)))
    hidden = (raw + raw * bent).astype(BF16)
    if pieces:
        pieces[1].wait()
    placed = (first + 0.5 * dot(hidden, down[...])).astype(BF16)
    normed = rms_rows(placed.astype(F32)).astype(BF16)
    keys_values = dot(normed, w_qkv[:, D:]).astype(BF16)
    state = jnp.concatenate(own_state(keys_values, by_row), axis=0)
    return placed, normed, keys_values, kept, state


def last(placed, carrying, summed, entering, w_out):
    mixed = dot(attended(carrying, summed, entering), w_out[...])
    return (placed[...].astype(F32) + mixed).astype(BF16)


def kernel_call(function, outs, *args, scalars=0, loose=(), outside=(), streamed=(), scratch=()):
    if DIRECT:
        return function(*args)
    count = len(args)

    def body(*refs):
        results = function(*refs[:count], *refs[count + len(outs) :])
        if len(outs) == 1:
            results = (results,)
        for ref, value in zip(refs[count:], results):
            ref[...] = value

    def spec(k):
        if k < scalars:
            return pl.BlockSpec(memory_space=pltpu.SMEM)
        return pl.BlockSpec(memory_space=pltpu.HBM if k in streamed else pltpu.VMEM)

    args = [
        arg
        if k < scalars or k in loose
        else pltpu.with_memory_space_constraint(
            arg, pltpu.HBM if k in streamed + outside else pltpu.VMEM
        )
        for k, arg in enumerate(args)
    ]
    result = pl.pallas_call(
        body,
        compiler_params=pltpu.CompilerParams(vmem_limit_bytes=32 << 20),
        out_shape=[jax.ShapeDtypeStruct(shape, kind) for shape, kind in outs],
        in_specs=[spec(k) for k in range(count)],
        out_specs=[pl.BlockSpec(memory_space=pltpu.VMEM)] * len(outs),
        scratch_shapes=list(scratch),
        name=function.__name__,
    )(*args)
    return result[0] if len(outs) == 1 else result


def whole(x, axes, pieces):
    split = x.reshape(pieces, x.shape[0] // pieces, x.shape[1])
    return lax.all_to_all(split, axes, split_axis=0, concat_axis=0, tiled=True).reshape(x.shape)


def shards(
    points,
    decay_one,
    decay_two,
    block_target,
    w_qkv_one,
    w_out_one,
    w_up,
    w_down,
    w_qkv_two,
    w_out_two,
):
    position = lax.axis_index(SEQ)
    member = position & 3
    limits = CAP * (position - member + iota((5, 1), 0))
    starts = jnp.sum((block_target[None, :] < limits).astype(jnp.int32), axis=1)
    meta = jnp.concatenate([starts, member[None].astype(jnp.int32)])
    own = lax.dynamic_slice_in_dim(block_target, position * 16, 16)
    fours = jnp.repeat(own // (4 * CAP), BR)[None, :]

    normed, keys_values, sent = kernel_call(
        front,
        [((128, D), BF16), ((128, 2 * D), BF16), ((1536, 128), BF16)],
        position[None].astype(jnp.int32),
        points,
        w_qkv_one,
        decay_one,
        w_up.T,
        w_down,
        decay_two,
        block_target.reshape(16, 128),
        scalars=1,
        outside=(1, 3, 4, 5, 6, 7),
        streamed=(2,),
        scratch=(pltpu.VMEM((D, 2 * D), BF16), pltpu.SemaphoreType.DMA((1,))),
    )
    received = lax.all_to_all(
        sent.reshape(384, 4, 128), SEQ, split_axis=0, concat_axis=0, tiled=True
    ).reshape(1536, 128)
    heads, column = kernel_call(sort, [((512, 128), BF16), ((128, 2 * D), BF16)], received)
    weights = lax.all_gather(column, ROW, axis=0, tiled=True)
    summed = kernel_call(prefix, [((256, 128), BF16)], heads)
    device_weight = kernel_call(later_weights, [((256, 256), BF16)], heads)
    own_rows = kernel_call(
        inner,
        [((128, D), BF16), ((128, D), F32)],
        normed,
        w_qkv_one,
        keys_values,
        decay_one,
        loose=(0, 2, 3),
        outside=(1,),
    )
    entering = whole(summed, SEQ, 128)
    outgoing = kernel_call(
        middle, [((256, D), BF16)], fours, points, *own_rows, entering, w_out_one
    )
    arrived = whole(outgoing, GROUPS, 32)
    outgoing = kernel_call(across, [((256, D), BF16)], meta, arrived, scalars=1)
    arrived = whole(outgoing, INSIDE, 4)
    placed, normed, keys_values, decay, sent = kernel_call(
        second,
        [
            ((256, D), BF16),
            ((256, D), BF16),
            ((256, 2 * D), BF16),
            ((HEADS, 256), F32),
            ((256, 128), BF16),
        ],
        meta,
        arrived,
        w_qkv_two,
        decay_two,
        weights,
        scalars=1,
        streamed=(4,),
        scratch=(
            pltpu.VMEM((4 * D, D), BF16),
            pltpu.VMEM((4 * D, D), BF16),
            pltpu.SemaphoreType.DMA((2,)),
        ),
    )
    received = whole(sent, SEQ, 128)
    own_rows = kernel_call(
        inner,
        [((256, D), BF16), ((256, D), F32)],
        normed,
        w_qkv_two,
        keys_values,
        decay,
        loose=(0, 2, 3),
        outside=(1,),
    )
    summed = kernel_call(later_prefix, [((256, 128), BF16)], received, device_weight)
    entering = whole(summed, SEQ, 128)
    return kernel_call(last, [((256, D), BF16)], placed, *own_rows, entering, w_out_two)


def solution(mesh):
    split = Mesh(
        mesh.devices.reshape(8, 4, 2, 2, mesh.shape["rep"]), SEQ + ("rep",)
    )
    placed = (
        P(REP_SEQ, None),
        P(None, REP_SEQ),
        P(None, REP_SEQ),
        P("rep"),
        P(),
        P(),
        P(None, SEQ),
        P(SEQ, None),
        P(),
        P(),
    )
    return jax.shard_map(
        shards, mesh=split, in_specs=placed, out_specs=P(REP_SEQ, None), check_vma=False
    )
```

```python
import math

import jax
import jax.numpy as jnp
from jax import lax
from jax.experimental import pallas as pl
from jax.experimental.pallas import tpu as pltpu
from jax.sharding import Mesh
from jax.sharding import PartitionSpec as P

D = 512
HEADS = 8
HEAD_DIM = 64
PAIRS = HEADS // 2
BR = 8
CAP = 32
SEQ = ("seq_0", "seq_1", "seq_2", "seq_3")
GROUPS = ("seq_0", "seq_1")
INSIDE = ("seq_2", "seq_3")
ROW = ("seq_1", "seq_2", "seq_3")
REP_SEQ = ("rep",) + SEQ
EPS = 1e-05
GELU = (2.0 / math.pi) ** 0.5
F32 = jnp.float32
BF16 = jnp.bfloat16
DIRECT = False

NN = (((1,), (0,)), ((), ()))
NT = (((1,), (1,)), ((), ()))
TN = (((0,), (0,)), ((), ()))


def dot(a, b, dims=NN):
    return lax.dot_general(a, b, dims, preferred_element_type=F32)


def iota(shape, dim):
    return lax.broadcasted_iota(jnp.int32, shape, dim)


def ones_where(cond):
    return jnp.where(cond, 1.0, 0.0).astype(BF16)


def halves(x):
    high = x.astype(BF16)
    return high, (x - high.astype(F32)).astype(BF16)


def thirds(x):
    high, rest = x.astype(BF16), x - x.astype(BF16).astype(F32)
    middle, low = halves(rest)
    return high, middle, low


def rms_rows(wide):
    return wide * lax.rsqrt(jnp.mean(wide * wide, axis=-1, keepdims=True) + EPS)


def running_sums(decay):
    rows = decay.shape[1]
    parts = thirds(decay)
    upto = ones_where(iota((rows, rows), 0) >= iota((rows, rows), 1))
    by_head = sum(dot(part, upto, NT) for part in parts)
    by_row = sum(dot(upto, part, NT) for part in parts)
    return by_head, by_row


def pair_lanes(columns, pair):
    rows = columns.shape[0]
    first = iota((rows, 2 * HEAD_DIM), 1) < HEAD_DIM
    return jnp.where(
        first, columns[:, 2 * pair : 2 * pair + 1], columns[:, 2 * pair + 1 : 2 * pair + 2]
    )


def own_state(keys_values, by_row):
    rows = keys_values.shape[0]
    weight = jnp.exp(by_row[rows - 1 : rows] - by_row)
    lane = iota((HEAD_DIM, 128), 1)
    states = []
    for p in range(PAIRS):
        keys = keys_values[:, 128 * p : 128 * (p + 1)].astype(F32) * pair_lanes(weight, p)
        values = keys_values[:, D + 128 * p : D + 128 * (p + 1)]
        both = dot(keys.astype(BF16), values, TN)
        states.append(jnp.where(lane < HEAD_DIM, both[:HEAD_DIM], both[HEAD_DIM:]).astype(BF16))
    return states


def pack(states, totals, more):
    place, column = iota((384, 128), 0), iota((384, 128), 1)
    device = (place * 43691) >> 19
    kind = place - 12 * device
    spread = ones_where((kind < 2) & (column == 2 * device + kind))[:, :HEAD_DIM]
    chosen = (kind >= 4) & (column == (kind - 4) * 16 + (device & 15))
    more = dot(ones_where(chosen), more)
    even = (iota((1, 128), 1) & 1) == 0
    packed = []
    for p in range(PAIRS):
        total = jnp.where(even, pair_lanes(totals[0], p), pair_lanes(totals[1], p))
        high, low = halves(total)
        piece = dot(spread, states[p]) + more
        piece = jnp.where(kind == 2, high.astype(F32), piece)
        piece = jnp.where(kind == 3, low.astype(F32), piece)
        packed.append(piece.astype(BF16))
    return jnp.concatenate(packed, axis=0)


def front(here, points, weight, decay, up, down, later, target):
    normed = rms_rows(points[...].astype(F32)).astype(BF16)
    keys_values = dot(normed, weight[:, D:]).astype(BF16)
    by_row = running_sums(decay[...])[1]
    used = jnp.where((target[...] >> 5) == here[0], 1.0, 0.0)
    used = jnp.sum(jnp.sum(used, axis=0, keepdims=True), axis=1, keepdims=True)
    kept = jnp.where(iota(later.shape, 1).astype(F32) < BR * used, later[...], 0.0)
    ones = ones_where(iota(later.shape, 0) >= 0)
    second_total = sum(dot(ones, part, NT) for part in thirds(kept))[:1]
    totals = (by_row[by_row.shape[0] - 1 :], second_total)
    more = [part[:, 128 * k : 128 * (k + 1)] for part in (up, down) for k in range(4)]
    more = jnp.concatenate(more, axis=0)
    return normed, keys_values, pack(own_state(keys_values, by_row), totals, more)


def sort(received):
    block = (192, 192)
    kind, device = iota(block, 0) >> 4, iota(block, 0) & 15
    order = ones_where(iota(block, 1) == 12 * device + kind)
    blocks = [dot(order, received[192 * g : 192 * (g + 1), :]).astype(BF16) for g in range(8)]

    def rows_of(kind):
        return jnp.concatenate([block[16 * kind : 16 * (kind + 1)] for block in blocks], axis=0)

    return (
        jnp.concatenate([rows_of(kind) for kind in range(4)], axis=0),
        jnp.concatenate([rows_of(kind) for kind in range(4, 12)], axis=1),
    )


def device_weights(heads, layer):
    square = (128, 128)
    earlier = iota(square, 1) < iota(square, 0)
    later = iota(square, 0) > iota(square, 1)
    before = ones_where(earlier)
    before = jnp.concatenate([before, before], axis=1)
    weights = []
    for half in range(2):
        at = half * HEAD_DIM + layer
        parts = [
            jnp.where(later, heads[128 * k : 128 * (k + 1), at : at + 1].astype(F32), 0.0)
            for k in (2, 3)
        ]
        gap = dot(before, jnp.concatenate(parts, axis=0).astype(BF16))
        high, low = halves(jnp.where(earlier, jnp.exp(gap), 0.0))
        weights.append(jnp.concatenate([high, low], axis=1))
    return weights


def gather_earlier(weights, states):
    both = jnp.concatenate([states, states], axis=0)
    outs = [dot(weight, both) for weight in weights]
    lane = iota(outs[0].shape, 1) & 127
    out = jnp.where(lane < HEAD_DIM, outs[0], outs[1]).astype(BF16)
    out = jnp.concatenate([out[:, :128], out[:, 128:]], axis=0)
    place, column = iota((256, 256), 0), iota((256, 256), 1)
    back = ones_where(column == (place & 1) * 128 + (place >> 1))
    return dot(back, out).astype(BF16)


def prefix(heads):
    states = jnp.concatenate([heads[:128, :], heads[128:256, :]], axis=1)
    return gather_earlier(device_weights(heads, 0), states)


def later_weights(heads):
    return jnp.concatenate(device_weights(heads, 1), axis=0)


def later_prefix(received, weights):
    place, column = iota((256, 256), 0), iota((256, 256), 1)
    order = ones_where(column == 2 * (place & 127) + (place >> 7))
    rows = dot(order, received[...]).astype(BF16)
    states = jnp.concatenate([rows[:128], rows[128:]], axis=1)
    return gather_earlier([weights[:128, :], weights[128:, :]], states)


def inner(normed, weight, keys_values, decay):
    by_head, by_row = running_sums(decay[...])
    queries = (dot(normed[...], weight[:, :D]) * HEAD_DIM ** (-0.5)).astype(BF16)
    rows = queries.shape[0]
    causal = iota((rows, rows), 0) >= iota((rows, rows), 1)
    lanes = iota((1, 128), 1)
    sides = (ones_where(lanes < HEAD_DIM), ones_where(lanes >= HEAD_DIM))
    first = iota((rows, 128), 1) < HEAD_DIM
    summed = []
    for p in range(PAIRS):
        query = queries[:, 128 * p : 128 * (p + 1)]
        keys = keys_values[:, 128 * p : 128 * (p + 1)]
        values = keys_values[:, D + 128 * p : D + 128 * (p + 1)]
        both = []
        for side in range(2):
            h = 2 * p + side
            scores = dot(query * sides[side], keys, NT)
            gap = by_row[:, h : h + 1] - by_head[h : h + 1, :]
            weighted = scores * jnp.exp(jnp.where(causal, gap, -1e30))
            both.append(dot(weighted.astype(BF16), values))
        summed.append(jnp.where(first, both[0], both[1]))
    grown = jnp.exp(by_row)
    carrying = [
        queries[:, 128 * p : 128 * (p + 1)].astype(F32) * pair_lanes(grown, p)
        for p in range(PAIRS)
    ]
    return jnp.concatenate(carrying, axis=1).astype(BF16), jnp.concatenate(summed, axis=1)


def attended(carrying, summed, entering):
    lanes = iota((1, 128), 1)
    sides = (ones_where(lanes < HEAD_DIM), ones_where(lanes >= HEAD_DIM))
    same = ones_where(iota((128, 128), 0) // HEAD_DIM == iota((128, 128), 1) // HEAD_DIM)
    outs = []
    for p in range(PAIRS):
        state = entering[HEAD_DIM * p : HEAD_DIM * (p + 1), :]
        state = jnp.concatenate([state * sides[0], state * sides[1]], axis=0)
        number = summed[:, 128 * p : 128 * (p + 1)]
        number = number + dot(carrying[:, 128 * p : 128 * (p + 1)], state)
        mean = dot((number * number).astype(BF16), same) * (1.0 / HEAD_DIM)
        outs.append((number * lax.rsqrt(mean + EPS)).astype(BF16))
    return jnp.concatenate(outs, axis=1)


def middle(fours, points, carrying, summed, entering, w_out):
    mixed = dot(attended(carrying, summed, entering), w_out[...])
    first = (points[...].astype(F32) + mixed).astype(BF16)
    shape = (256, 128)
    place, column = iota(shape, 0), iota(shape, 1)
    chosen = (place // BR == fours[...]) & ((place & 7) == (column & 7))
    return dot(ones_where(chosen), first).astype(BF16)


def across(meta, arrived):
    shape = (256, 256)
    place, column = iota(shape, 0), iota(shape, 1)
    begin = sum(jnp.where(place // 64 == k, meta[k], 0) for k in range(4))
    end = sum(jnp.where(place // 64 == k, meta[k + 1], 0) for k in range(4))
    where = begin + ((meta[5] - begin) & 3) + 4 * ((place // BR) & 7)
    held = (where & 127) >> 2
    chosen = (where < end) & (column == held * BR + (place & 7))
    return dot(ones_where(chosen), arrived[...]).astype(BF16)


def arrive(meta, arrived, decay):
    shape = (256, 256)
    place, column = iota(shape, 0), iota(shape, 1)
    begin = meta[meta[5]]
    used = meta[meta[5] + 1] - begin
    slot = place // BR
    held = ((begin + slot) & 3) * 8 + slot // 4
    chosen = (slot < used) & (column == held * BR + (place & 7))
    first = dot(ones_where(chosen), arrived[...])
    kept = jnp.where(iota(decay.shape, 1) < BR * used, decay[...], 0.0)
    return first.astype(BF16), rms_rows(first).astype(BF16), kept, running_sums(kept)[1]


def second(first, normed, by_row, w_qkv, weights, up=None, down=None, copies=None):
    pieces = []
    if up is None:
        up, down = weights[:, :D], weights[:, D:]
    else:
        for k, buffer in enumerate((up, down)):
            pieces.append(
                pltpu.make_async_copy(weights.at[:, pl.ds(k * D, D)], buffer, copies.at[k])
            )
            pieces[k].start()
    if pieces:
        pieces[0].wait()
    raw = dot(normed[...], up[...], NT)
    bent = jnp.tanh(raw * (GELU + (GELU * 0.044715) * (raw * raw)))
    hidden = (raw + raw * bent).astype(BF16)
    if pieces:
        pieces[1].wait()
    placed = (first[...].astype(F32) + 0.5 * dot(hidden, down[...])).astype(BF16)
    normed = rms_rows(placed.astype(F32)).astype(BF16)
    keys_values = dot(normed, w_qkv[:, D:]).astype(BF16)
    state = jnp.concatenate(own_state(keys_values, by_row[...]), axis=0)
    return placed, normed, keys_values, state


def last(placed, carrying, summed, entering, w_out):
    mixed = dot(attended(carrying, summed, entering), w_out[...])
    return (placed[...].astype(F32) + mixed).astype(BF16)


def kernel_call(function, outs, *args, scalars=0, loose=(), outside=(), streamed=(), scratch=()):
    if DIRECT:
        return function(*args)
    count = len(args)

    def body(*refs):
        results = function(*refs[:count], *refs[count + len(outs) :])
        if len(outs) == 1:
            results = (results,)
        for ref, value in zip(refs[count:], results):
            ref[...] = value

    def spec(k):
        if k < scalars:
            return pl.BlockSpec(memory_space=pltpu.SMEM)
        return pl.BlockSpec(memory_space=pltpu.HBM if k in streamed else pltpu.VMEM)

    args = [
        arg
        if k < scalars or k in loose
        else pltpu.with_memory_space_constraint(
            arg, pltpu.HBM if k in streamed + outside else pltpu.VMEM
        )
        for k, arg in enumerate(args)
    ]
    result = pl.pallas_call(
        body,
        compiler_params=pltpu.CompilerParams(vmem_limit_bytes=32 << 20),
        out_shape=[jax.ShapeDtypeStruct(shape, kind) for shape, kind in outs],
        in_specs=[spec(k) for k in range(count)],
        out_specs=[pl.BlockSpec(memory_space=pltpu.VMEM)] * len(outs),
        scratch_shapes=list(scratch),
        name=function.__name__,
    )(*args)
    return result[0] if len(outs) == 1 else result


def whole(x, axes, pieces):
    split = x.reshape(pieces, x.shape[0] // pieces, x.shape[1])
    return lax.all_to_all(split, axes, split_axis=0, concat_axis=0, tiled=True).reshape(x.shape)


def shards(
    points,
    decay_one,
    decay_two,
    block_target,
    w_qkv_one,
    w_out_one,
    w_up,
    w_down,
    w_qkv_two,
    w_out_two,
):
    position = lax.axis_index(SEQ)
    member = position & 3
    limits = CAP * (position - member + iota((5, 1), 0))
    starts = jnp.sum((block_target[None, :] < limits).astype(jnp.int32), axis=1)
    meta = jnp.concatenate([starts, member[None].astype(jnp.int32)])
    own = lax.dynamic_slice_in_dim(block_target, position * 16, 16)
    fours = jnp.repeat(own // (4 * CAP), BR)[None, :]

    normed, keys_values, sent = kernel_call(
        front,
        [((128, D), BF16), ((128, 2 * D), BF16), ((1536, 128), BF16)],
        position[None].astype(jnp.int32),
        points,
        w_qkv_one,
        decay_one,
        w_up.T,
        w_down,
        decay_two,
        block_target.reshape(16, 128),
        scalars=1,
        outside=(1, 2, 3, 4, 5, 6, 7),
    )
    received = lax.all_to_all(
        sent.reshape(384, 4, 128), SEQ, split_axis=0, concat_axis=0, tiled=True
    ).reshape(1536, 128)
    heads, column = kernel_call(sort, [((512, 128), BF16), ((128, 2 * D), BF16)], received)
    weights = lax.all_gather(column, ROW, axis=0, tiled=True)
    summed = kernel_call(prefix, [((256, 128), BF16)], heads)
    device_weight = kernel_call(later_weights, [((256, 256), BF16)], heads)
    own_rows = kernel_call(
        inner,
        [((128, D), BF16), ((128, D), F32)],
        normed,
        w_qkv_one,
        keys_values,
        decay_one,
        loose=(0, 2, 3),
        outside=(1,),
    )
    entering = whole(summed, SEQ, 128)
    outgoing = kernel_call(
        middle, [((256, D), BF16)], fours, points, *own_rows, entering, w_out_one
    )
    arrived = whole(outgoing, GROUPS, 32)
    outgoing = kernel_call(across, [((256, D), BF16)], meta, arrived, scalars=1)
    arrived = whole(outgoing, INSIDE, 4)
    first, normed, decay, by_row = kernel_call(
        arrive,
        [((256, D), BF16), ((256, D), BF16), ((HEADS, 256), F32), ((256, HEADS), F32)],
        meta,
        arrived,
        decay_two,
        scalars=1,
    )
    first, weights = lax.optimization_barrier((first, weights))
    placed, normed, keys_values, sent = kernel_call(
        second,
        [((256, D), BF16), ((256, D), BF16), ((256, 2 * D), BF16), ((256, 128), BF16)],
        first,
        normed,
        by_row,
        w_qkv_two,
        weights,
        streamed=(4,),
        scratch=(
            pltpu.VMEM((4 * D, D), BF16),
            pltpu.VMEM((4 * D, D), BF16),
            pltpu.SemaphoreType.DMA((2,)),
        ),
    )
    received = whole(sent, SEQ, 128)
    own_rows = kernel_call(
        inner,
        [((256, D), BF16), ((256, D), F32)],
        normed,
        w_qkv_two,
        keys_values,
        decay,
        loose=(0, 2, 3),
        outside=(1,),
    )
    summed = kernel_call(later_prefix, [((256, 128), BF16)], received, device_weight)
    entering = whole(summed, SEQ, 128)
    return kernel_call(last, [((256, D), BF16)], placed, *own_rows, entering, w_out_two)


def solution(mesh):
    split = Mesh(
        mesh.devices.reshape(8, 4, 2, 2, mesh.shape["rep"]), SEQ + ("rep",)
    )
    placed = (
        P(REP_SEQ, None),
        P(None, REP_SEQ),
        P(None, REP_SEQ),
        P("rep"),
        P(),
        P(),
        P(None, SEQ),
        P(SEQ, None),
        P(),
        P(),
    )
    return jax.shard_map(
        shards, mesh=split, in_specs=placed, out_specs=P(REP_SEQ, None), check_vma=False
    )
```

```python
import math

import jax
import jax.numpy as jnp
from jax import lax
from jax.experimental import pallas as pl
from jax.experimental.pallas import tpu as pltpu
from jax.sharding import Mesh
from jax.sharding import PartitionSpec as P

D = 512
HEADS = 8
HEAD_DIM = 64
PAIRS = HEADS // 2
BR = 8
CAP = 32
SEQ = ("seq_0", "seq_1", "seq_2", "seq_3")
GROUPS = ("seq_0", "seq_1")
INSIDE = ("seq_2", "seq_3")
ROW = ("seq_1", "seq_2", "seq_3")
REP_SEQ = ("rep",) + SEQ
EPS = 1e-05
GELU = (2.0 / math.pi) ** 0.5
F32 = jnp.float32
BF16 = jnp.bfloat16
DIRECT = False

NN = (((1,), (0,)), ((), ()))
NT = (((1,), (1,)), ((), ()))
TN = (((0,), (0,)), ((), ()))


def dot(a, b, dims=NN):
    return lax.dot_general(a, b, dims, preferred_element_type=F32)


def iota(shape, dim):
    return lax.broadcasted_iota(jnp.int32, shape, dim)


def ones_where(cond):
    return jnp.where(cond, 1.0, 0.0).astype(BF16)


def halves(x):
    high = x.astype(BF16)
    return high, (x - high.astype(F32)).astype(BF16)


def thirds(x):
    high, rest = x.astype(BF16), x - x.astype(BF16).astype(F32)
    middle, low = halves(rest)
    return high, middle, low


def rms_rows(wide):
    return wide * lax.rsqrt(jnp.mean(wide * wide, axis=-1, keepdims=True) + EPS)


def running_sums(decay):
    rows = decay.shape[1]
    parts = thirds(decay)
    upto = ones_where(iota((rows, rows), 0) >= iota((rows, rows), 1))
    by_head = sum(dot(part, upto, NT) for part in parts)
    by_row = sum(dot(upto, part, NT) for part in parts)
    return by_head, by_row


def pair_lanes(columns, pair):
    rows = columns.shape[0]
    first = iota((rows, 2 * HEAD_DIM), 1) < HEAD_DIM
    return jnp.where(
        first, columns[:, 2 * pair : 2 * pair + 1], columns[:, 2 * pair + 1 : 2 * pair + 2]
    )


def own_state(keys_values, by_row):
    rows = keys_values.shape[0]
    weight = jnp.exp(by_row[rows - 1 : rows] - by_row)
    lane = iota((HEAD_DIM, 128), 1)
    states = []
    for p in range(PAIRS):
        keys = keys_values[:, 128 * p : 128 * (p + 1)].astype(F32) * pair_lanes(weight, p)
        values = keys_values[:, D + 128 * p : D + 128 * (p + 1)]
        both = dot(keys.astype(BF16), values, TN)
        states.append(jnp.where(lane < HEAD_DIM, both[:HEAD_DIM], both[HEAD_DIM:]).astype(BF16))
    return states


def pack(states, totals, more):
    place, column = iota((384, 128), 0), iota((384, 128), 1)
    device = (place * 43691) >> 19
    kind = place - 12 * device
    spread = ones_where((kind < 2) & (column == 2 * device + kind))[:, :HEAD_DIM]
    chosen = (kind >= 4) & (column == (kind - 4) * 16 + (device & 15))
    more = dot(ones_where(chosen), more)
    even = (iota((1, 128), 1) & 1) == 0
    packed = []
    for p in range(PAIRS):
        total = jnp.where(even, pair_lanes(totals[0], p), pair_lanes(totals[1], p))
        high, low = halves(total)
        piece = dot(spread, states[p]) + more
        piece = jnp.where(kind == 2, high.astype(F32), piece)
        piece = jnp.where(kind == 3, low.astype(F32), piece)
        packed.append(piece.astype(BF16))
    return jnp.concatenate(packed, axis=0)


def front(here, points, weight, decay, up, down, later, target):
    normed = rms_rows(points[...].astype(F32)).astype(BF16)
    keys_values = dot(normed, weight[:, D:]).astype(BF16)
    by_row = running_sums(decay[...])[1]
    used = jnp.where((target[...] >> 5) == here[0], 1.0, 0.0)
    used = jnp.sum(jnp.sum(used, axis=0, keepdims=True), axis=1, keepdims=True)
    kept = jnp.where(iota(later.shape, 1).astype(F32) < BR * used, later[...], 0.0)
    ones = ones_where(iota(later.shape, 0) >= 0)
    second_total = sum(dot(ones, part, NT) for part in thirds(kept))[:1]
    totals = (by_row[by_row.shape[0] - 1 :], second_total)
    more = [part[:, 128 * k : 128 * (k + 1)] for part in (up, down) for k in range(4)]
    more = jnp.concatenate(more, axis=0)
    return normed, keys_values, pack(own_state(keys_values, by_row), totals, more)


def sort(received):
    block = (192, 192)
    kind, device = iota(block, 0) >> 4, iota(block, 0) & 15
    order = ones_where(iota(block, 1) == 12 * device + kind)
    blocks = [dot(order, received[192 * g : 192 * (g + 1), :]).astype(BF16) for g in range(8)]

    def rows_of(kind):
        return jnp.concatenate([block[16 * kind : 16 * (kind + 1)] for block in blocks], axis=0)

    return (
        jnp.concatenate([rows_of(kind) for kind in range(4)], axis=0),
        jnp.concatenate([rows_of(kind) for kind in range(4, 12)], axis=1),
    )


def device_weights(heads, layer):
    square = (128, 128)
    earlier = iota(square, 1) < iota(square, 0)
    later = iota(square, 0) > iota(square, 1)
    before = ones_where(earlier)
    before = jnp.concatenate([before, before], axis=1)
    weights = []
    for half in range(2):
        at = half * HEAD_DIM + layer
        parts = [
            jnp.where(later, heads[128 * k : 128 * (k + 1), at : at + 1].astype(F32), 0.0)
            for k in (2, 3)
        ]
        gap = dot(before, jnp.concatenate(parts, axis=0).astype(BF16))
        high, low = halves(jnp.where(earlier, jnp.exp(gap), 0.0))
        weights.append(jnp.concatenate([high, low], axis=1))
    return weights


def gather_earlier(weights, states):
    both = jnp.concatenate([states, states], axis=0)
    outs = [dot(weight, both) for weight in weights]
    lane = iota(outs[0].shape, 1) & 127
    out = jnp.where(lane < HEAD_DIM, outs[0], outs[1]).astype(BF16)
    out = jnp.concatenate([out[:, :128], out[:, 128:]], axis=0)
    place, column = iota((256, 256), 0), iota((256, 256), 1)
    back = ones_where(column == (place & 1) * 128 + (place >> 1))
    return dot(back, out).astype(BF16)


def prefix(heads):
    states = jnp.concatenate([heads[:128, :], heads[128:256, :]], axis=1)
    return gather_earlier(device_weights(heads, 0), states)


def later_weights(heads):
    return jnp.concatenate(device_weights(heads, 1), axis=0)


def later_prefix(received, weights):
    place, column = iota((256, 256), 0), iota((256, 256), 1)
    order = ones_where(column == 2 * (place & 127) + (place >> 7))
    rows = dot(order, received[...]).astype(BF16)
    states = jnp.concatenate([rows[:128], rows[128:]], axis=1)
    return gather_earlier([weights[:128, :], weights[128:, :]], states)


def inner(normed, weight, keys_values, decay):
    by_head, by_row = running_sums(decay[...])
    queries = (dot(normed[...], weight[:, :D]) * HEAD_DIM ** (-0.5)).astype(BF16)
    rows = queries.shape[0]
    causal = iota((rows, rows), 0) >= iota((rows, rows), 1)
    lanes = iota((1, 128), 1)
    sides = (ones_where(lanes < HEAD_DIM), ones_where(lanes >= HEAD_DIM))
    first = iota((rows, 128), 1) < HEAD_DIM
    summed = []
    for p in range(PAIRS):
        query = queries[:, 128 * p : 128 * (p + 1)]
        keys = keys_values[:, 128 * p : 128 * (p + 1)]
        values = keys_values[:, D + 128 * p : D + 128 * (p + 1)]
        both = []
        for side in range(2):
            h = 2 * p + side
            scores = dot(query * sides[side], keys, NT)
            gap = by_row[:, h : h + 1] - by_head[h : h + 1, :]
            weighted = scores * jnp.exp(jnp.where(causal, gap, -1e30))
            both.append(dot(weighted.astype(BF16), values))
        summed.append(jnp.where(first, both[0], both[1]))
    grown = jnp.exp(by_row)
    carrying = [
        queries[:, 128 * p : 128 * (p + 1)].astype(F32) * pair_lanes(grown, p)
        for p in range(PAIRS)
    ]
    return jnp.concatenate(carrying, axis=1).astype(BF16), jnp.concatenate(summed, axis=1)


def attended(carrying, summed, entering):
    lanes = iota((1, 128), 1)
    sides = (ones_where(lanes < HEAD_DIM), ones_where(lanes >= HEAD_DIM))
    same = ones_where(iota((128, 128), 0) // HEAD_DIM == iota((128, 128), 1) // HEAD_DIM)
    outs = []
    for p in range(PAIRS):
        state = entering[HEAD_DIM * p : HEAD_DIM * (p + 1), :]
        state = jnp.concatenate([state * sides[0], state * sides[1]], axis=0)
        number = summed[:, 128 * p : 128 * (p + 1)]
        number = number + dot(carrying[:, 128 * p : 128 * (p + 1)], state)
        mean = dot((number * number).astype(BF16), same) * (1.0 / HEAD_DIM)
        outs.append((number * lax.rsqrt(mean + EPS)).astype(BF16))
    return jnp.concatenate(outs, axis=1)


def middle(fours, points, carrying, summed, entering, w_out):
    mixed = dot(attended(carrying, summed, entering), w_out[...])
    first = (points[...].astype(F32) + mixed).astype(BF16)
    shape = (256, 128)
    place, column = iota(shape, 0), iota(shape, 1)
    chosen = (place // BR == fours[...]) & ((place & 7) == (column & 7))
    return dot(ones_where(chosen), first).astype(BF16)


def across(meta, arrived):
    shape = (256, 256)
    place, column = iota(shape, 0), iota(shape, 1)
    begin = sum(jnp.where(place // 64 == k, meta[k], 0) for k in range(4))
    end = sum(jnp.where(place // 64 == k, meta[k + 1], 0) for k in range(4))
    where = begin + ((meta[5] - begin) & 3) + 4 * ((place // BR) & 7)
    held = (where & 127) >> 2
    chosen = (where < end) & (column == held * BR + (place & 7))
    return dot(ones_where(chosen), arrived[...]).astype(BF16)


def arrive(meta, arrived, decay):
    shape = (256, 256)
    place, column = iota(shape, 0), iota(shape, 1)
    begin = meta[meta[5]]
    used = meta[meta[5] + 1] - begin
    slot = place // BR
    held = ((begin + slot) & 3) * 8 + slot // 4
    chosen = (slot < used) & (column == held * BR + (place & 7))
    first = dot(ones_where(chosen), arrived[...])
    kept = jnp.where(iota(decay.shape, 1) < BR * used, decay[...], 0.0)
    return first.astype(BF16), rms_rows(first).astype(BF16), kept, running_sums(kept)[1]


def second(first, normed, by_row, w_qkv, weights, up=None, down=None, copies=None):
    pieces = []
    if up is None:
        up, down = weights[:, :D], weights[:, D:]
    else:
        for k, buffer in enumerate((up, down)):
            pieces.append(
                pltpu.make_async_copy(weights.at[:, pl.ds(k * D, D)], buffer, copies.at[k])
            )
            pieces[k].start()
    if pieces:
        pieces[0].wait()
    raw = dot(normed[...], up[...], NT).astype(BF16)
    bent = jnp.tanh(raw * (GELU + (GELU * 0.044715) * (raw * raw)))
    hidden = raw + raw * bent
    if pieces:
        pieces[1].wait()
    placed = (first[...].astype(F32) + 0.5 * dot(hidden, down[...])).astype(BF16)
    normed = rms_rows(placed.astype(F32)).astype(BF16)
    keys_values = dot(normed, w_qkv[:, D:]).astype(BF16)
    state = jnp.concatenate(own_state(keys_values, by_row[...]), axis=0)
    return placed, normed, keys_values, state


def last(placed, carrying, summed, entering, w_out):
    mixed = dot(attended(carrying, summed, entering), w_out[...])
    return (placed[...].astype(F32) + mixed).astype(BF16)


def kernel_call(function, outs, *args, scalars=0, loose=(), outside=(), streamed=(), scratch=()):
    if DIRECT:
        return function(*args)
    count = len(args)

    def body(*refs):
        results = function(*refs[:count], *refs[count + len(outs) :])
        if len(outs) == 1:
            results = (results,)
        for ref, value in zip(refs[count:], results):
            ref[...] = value

    def spec(k):
        if k < scalars:
            return pl.BlockSpec(memory_space=pltpu.SMEM)
        return pl.BlockSpec(memory_space=pltpu.HBM if k in streamed else pltpu.VMEM)

    args = [
        arg
        if k < scalars or k in loose
        else pltpu.with_memory_space_constraint(
            arg, pltpu.HBM if k in streamed + outside else pltpu.VMEM
        )
        for k, arg in enumerate(args)
    ]
    result = pl.pallas_call(
        body,
        compiler_params=pltpu.CompilerParams(vmem_limit_bytes=32 << 20),
        out_shape=[jax.ShapeDtypeStruct(shape, kind) for shape, kind in outs],
        in_specs=[spec(k) for k in range(count)],
        out_specs=[pl.BlockSpec(memory_space=pltpu.VMEM)] * len(outs),
        scratch_shapes=list(scratch),
        name=function.__name__,
    )(*args)
    return result[0] if len(outs) == 1 else result


def whole(x, axes, pieces):
    split = x.reshape(pieces, x.shape[0] // pieces, x.shape[1])
    return lax.all_to_all(split, axes, split_axis=0, concat_axis=0, tiled=True).reshape(x.shape)


def shards(
    points,
    decay_one,
    decay_two,
    block_target,
    w_qkv_one,
    w_out_one,
    w_up,
    w_down,
    w_qkv_two,
    w_out_two,
):
    position = lax.axis_index(SEQ)
    member = position & 3
    limits = CAP * (position - member + iota((5, 1), 0))
    starts = jnp.sum((block_target[None, :] < limits).astype(jnp.int32), axis=1)
    meta = jnp.concatenate([starts, member[None].astype(jnp.int32)])
    own = lax.dynamic_slice_in_dim(block_target, position * 16, 16)
    fours = jnp.repeat(own // (4 * CAP), BR)[None, :]

    normed, keys_values, sent = kernel_call(
        front,
        [((128, D), BF16), ((128, 2 * D), BF16), ((1536, 128), BF16)],
        position[None].astype(jnp.int32),
        points,
        w_qkv_one,
        decay_one,
        w_up.T,
        w_down,
        decay_two,
        block_target.reshape(16, 128),
        scalars=1,
        outside=(1, 2, 3, 4, 5, 6, 7),
    )
    received = lax.all_to_all(
        sent.reshape(384, 4, 128), SEQ, split_axis=0, concat_axis=0, tiled=True
    ).reshape(1536, 128)
    heads, column = kernel_call(sort, [((512, 128), BF16), ((128, 2 * D), BF16)], received)
    weights = lax.all_gather(column, ROW, axis=0, tiled=True)
    summed = kernel_call(prefix, [((256, 128), BF16)], heads)
    device_weight = kernel_call(later_weights, [((256, 256), BF16)], heads)
    own_rows = kernel_call(
        inner,
        [((128, D), BF16), ((128, D), F32)],
        normed,
        w_qkv_one,
        keys_values,
        decay_one,
        loose=(0, 2, 3),
        outside=(1,),
    )
    entering = whole(summed, SEQ, 128)
    outgoing = kernel_call(
        middle, [((256, D), BF16)], fours, points, *own_rows, entering, w_out_one
    )
    arrived = whole(outgoing, GROUPS, 32)
    outgoing = kernel_call(across, [((256, D), BF16)], meta, arrived, scalars=1)
    arrived = whole(outgoing, INSIDE, 4)
    first, normed, decay, by_row = kernel_call(
        arrive,
        [((256, D), BF16), ((256, D), BF16), ((HEADS, 256), F32), ((256, HEADS), F32)],
        meta,
        arrived,
        decay_two,
        scalars=1,
    )
    first, weights = lax.optimization_barrier((first, weights))
    placed, normed, keys_values, sent = kernel_call(
        second,
        [((256, D), BF16), ((256, D), BF16), ((256, 2 * D), BF16), ((256, 128), BF16)],
        first,
        normed,
        by_row,
        w_qkv_two,
        weights,
        streamed=(4,),
        scratch=(
            pltpu.VMEM((4 * D, D), BF16),
            pltpu.VMEM((4 * D, D), BF16),
            pltpu.SemaphoreType.DMA((2,)),
        ),
    )
    received = whole(sent, SEQ, 128)
    own_rows = kernel_call(
        inner,
        [((256, D), BF16), ((256, D), F32)],
        normed,
        w_qkv_two,
        keys_values,
        decay,
        loose=(0, 2, 3),
        outside=(1,),
    )
    summed = kernel_call(later_prefix, [((256, 128), BF16)], received, device_weight)
    entering = whole(summed, SEQ, 128)
    return kernel_call(last, [((256, D), BF16)], placed, *own_rows, entering, w_out_two)


def solution(mesh):
    split = Mesh(
        mesh.devices.reshape(8, 4, 2, 2, mesh.shape["rep"]), SEQ + ("rep",)
    )
    placed = (
        P(REP_SEQ, None),
        P(None, REP_SEQ),
        P(None, REP_SEQ),
        P("rep"),
        P(),
        P(),
        P(None, SEQ),
        P(SEQ, None),
        P(),
        P(),
    )
    return jax.shard_map(
        shards, mesh=split, in_specs=placed, out_specs=P(REP_SEQ, None), check_vma=False
    )
```
